32 devices in a mesh: wave: 2 (over y), gy: 4 (over z), gz: 2 (over x), vec: 2 (over core).
Axes of the slice: x: 2, y: 2, z: 4, core: 2. Of those that a mesh axis runs over, the one named last changes fastest.
Arguments:
- forcing: float32 [8, 8, 512, 1024], P(('wave', 'vec'), None, 'gy', 'gz'), parts along dimension 0, may hold values from -6 to 6
- wavenumber: float32 [2], P('wave'), parts along dimension 0, may hold values from 0.5 to 2
- mean_flow: float32 [9, 512, 1024], P(None, 'gy', 'gz'), may hold values from -3 to 3
- viscosity: float32 [512, 1024], P('gy', 'gz'), may hold values from 0.05 to 0.5
- viscosity_slope: float32 [2, 512, 1024], P(None, 'gy', 'gz'), may hold values from -1.8 to 1.8
Outputs:
- response: float32 [8, 8, 512, 1024], P(('wave', 'vec'), None, 'gy', 'gz'), parts along dimension 0
The draws below stay inside these ranges and needn't reach their ends.
There are 2 independent parts, one for each index of `wave`. The reference program is written for one: setup_inputs(seed, part) draws one part's arguments, and reference() takes and returns one part's arrays. A program takes and returns all parts, laid end to end along the dimension named above; an argument that names none is the same for every part. Nothing has to cross between parts.
All inputs are finite; a program needn't handle non-finite values.
Results may differ from the reference program's by a relative error of at most 0.00005.
Values sent between devices are 32-bit elements; how exact they have to be, the bound alone decides.
No kernel may reach another device: no remote copies, remote signals or barrier semaphores. Data moves between devices by JAX's collectives and lax.ppermute only.
A program may use at most 128 MiB of HBM per device.

```python
import math
import jax
import jax.numpy as jnp
from jax import lax

VECS = 4
NY = 512
NZ = 1024


def block_scale(rng, shape, cuts, low, largest):
    level = 1.0
    for dim, shards_of in cuts:
        steps = jax.random.uniform(jax.random.fold_in(jax.random.fold_in(rng, 6), dim), (shards_of,), jnp.float32, low / len(cuts), largest / len(cuts))
        level = level * jnp.repeat(jnp.exp(steps), shape[dim] // shards_of).reshape((-1,) + (1,) * (len(shape) - 1 - dim))
    return level


def noise(stream_key, extent, scale, limit, pieces=(), kind=jnp.bfloat16):
    drawn = scale * jax.random.normal(stream_key, extent, jnp.float32)
    if pieces:
        drawn = drawn * block_scale(stream_key, extent, pieces, -0.22, 0.18)
    return jnp.clip(drawn, -limit, limit).astype(kind)


def setup_inputs(seed: int = 0, part: int = 0) -> dict:
    keys = jax.random.split(jax.random.key(seed), 6)
    part_keys = jax.random.split(jax.random.fold_in(keys[5], part), 6)
    return {
        "forcing": noise(part_keys[0], (VECS, 8, NY, NZ), 1.0, 6.0, ((0, 2), (2, 4), (3, 2)), jnp.float32),
        "wavenumber": jnp.clip(jax.random.uniform(part_keys[1], (1,), jnp.float32, 0.5, 2.0), 0.5, 2.0),
        "mean_flow": noise(keys[2], (9, NY, NZ), 0.5, 3.0, ((1, 4), (2, 2)), jnp.float32),
        "viscosity": jnp.clip(jnp.exp(math.log(0.5) - 2.3025851 * jax.random.uniform(keys[3], (NY, NZ), jnp.float32) ** block_scale(keys[3], (NY, NZ), ((0, 4), (1, 2)), -0.2, 0.2)), 0.05, 0.5),
        "viscosity_slope": noise(keys[4], (2, NY, NZ), 0.3, 1.8, ((1, 4), (2, 2)), jnp.float32),
    }


precise = lax.Precision.HIGHEST


def angle_table(points):
    last_index = points - 1
    row_index = jnp.arange(points, dtype=jnp.int32)[:, None]
    col_index = jnp.arange(points, dtype=jnp.int32)[None, :]
    unit = math.pi / (2.0 * last_index)
    sine_row = jnp.sin(2.0 * unit * jnp.minimum(row_index, last_index - row_index).astype(jnp.float32))
    total = row_index + col_index
    half_sum = jnp.sin(unit * jnp.minimum(total, 2 * last_index - total).astype(jnp.float32))
    half_diff = jnp.sin(unit * (row_index - col_index).astype(jnp.float32))
    parity = (1 - 2 * (total % 2)).astype(jnp.float32)
    weight = jnp.where((col_index == 0) | (col_index == last_index), 0.5, 1.0).astype(jnp.float32)
    same = row_index == col_index
    denominator = jnp.where(same, 1.0, 2.0 * half_sum * half_diff)
    offdiag = jnp.where(same, 0.0, (math.pi / last_index) * sine_row * parity * weight / denominator)
    diagonal = -jnp.sum(offdiag, axis=1)
    return offdiag + jnp.diag(diagonal)


def rotate(values):
    return jnp.stack((-values[..., 1, :, :], values[..., 0, :, :]), axis=-3)


def apply_operator(forcing, grad_y, curve_y, grad_z, curve_z, streamwise, mean_flow, viscosity, viscosity_slope):
    full_shape = forcing.shape
    split_shape = full_shape[:-3] + (4, 2) + full_shape[-2:]
    source = forcing.reshape(split_shape)
    grad_y = grad_y.reshape(split_shape)
    curve_y = curve_y.reshape(split_shape)
    grad_z = grad_z.reshape(split_shape)
    curve_z = curve_z.reshape(split_shape)
    velocity = source[..., :3, :, :, :]
    advection = streamwise * mean_flow[0] * rotate(velocity) + mean_flow[1] * grad_y[..., :3, :, :, :] + mean_flow[2] * grad_z[..., :3, :, :, :]
    slope_y = jnp.stack((mean_flow[3], mean_flow[5], mean_flow[7]))[:, None]
    slope_z = jnp.stack((mean_flow[4], mean_flow[6], mean_flow[8]))[:, None]
    produce = slope_y * source[..., 1:2, :, :, :] + slope_z * source[..., 2:3, :, :, :]
    diffuse = viscosity * (curve_y[..., :3, :, :, :] + curve_z[..., :3, :, :, :] - streamwise * streamwise * velocity)
    diffuse = diffuse + viscosity_slope[0] * grad_y[..., :3, :, :, :] + viscosity_slope[1] * grad_z[..., :3, :, :, :]
    pressure = jnp.stack((streamwise * rotate(source[..., 3, :, :, :]), grad_y[..., 3, :, :, :], grad_z[..., 3, :, :, :]), axis=-4)
    momentum = -advection - produce + diffuse - pressure
    continuity = streamwise * rotate(source[..., 0, :, :, :]) + grad_y[..., 1, :, :, :] + grad_z[..., 2, :, :, :]
    action = jnp.concatenate((momentum, continuity[..., None, :, :, :]), axis=-4)
    return action.reshape(full_shape)


def reference(forcing, wavenumber, mean_flow, viscosity, viscosity_slope):
    table_y = angle_table(NY)
    table_z = angle_table(NZ)
    streamwise = wavenumber[0]

    def one_vector(vector):
        grad_y = jnp.einsum('ij,cjz->ciz', table_y, vector, precision=precise)
        curve_y = jnp.einsum('ij,cjz->ciz', table_y, grad_y, precision=precise)
        grad_z = jnp.einsum('cyj,ij->cyi', vector, table_z, precision=precise)
        curve_z = jnp.einsum('cyj,ij->cyi', grad_z, table_z, precision=precise)
        return apply_operator(vector, grad_y, curve_y, grad_z, curve_z, streamwise, mean_flow, viscosity, viscosity_slope)

    action = lax.map(one_vector, forcing)
    y_signs = jnp.array([1.0, 1.0, -1.0, -1.0, 1.0, 1.0, 1.0, 1.0], dtype=jnp.float32)[:, None, None]
    z_signs = jnp.array([1.0, 1.0, 1.0, 1.0, -1.0, -1.0, 1.0, 1.0], dtype=jnp.float32)[:, None, None]
    half_y = 0.5 * (action + y_signs * jnp.flip(action, axis=-2))
    return 0.5 * (half_y + z_signs * jnp.flip(half_y, axis=-1))
```

```python
import functools
import math

import jax
import jax.numpy as jnp
import ml_dtypes
import numpy as np
from jax import lax
from jax.experimental import pallas as pl
from jax.experimental.pallas import tpu as pltpu
from jax.sharding import PartitionSpec as P


Y_SIGNS = (1.0, -1.0, 1.0, 1.0)
Z_SIGNS = (1.0, 1.0, -1.0, 1.0)
ROW_STEP = 16


def angle_table(points):
    last = points - 1
    row = np.arange(points)[:, None]
    col = np.arange(points)[None, :]
    unit = math.pi / (2.0 * last)
    sine_row = np.sin(2.0 * unit * np.minimum(row, last - row))
    total = row + col
    half_sum = np.sin(unit * np.minimum(total, 2 * last - total))
    half_diff = np.sin(unit * (row - col))
    parity = 1.0 - 2.0 * (total % 2)
    weight = np.where((col == 0) | (col == last), 0.5, 1.0)
    same = row == col
    denominator = np.where(same, 1.0, 2.0 * half_sum * half_diff)
    offdiag = np.where(same, 0.0, math.pi / last * sine_row * parity * weight / denominator)
    return offdiag - np.diag(offdiag.sum(axis=1))


def folded_tables(points):
    table = angle_table(points)
    second = table @ table
    half = points // 2
    stacked = np.concatenate(
        [part for full in (table, second) for part in (full[:half, :half], full[::-1][:half, :half])]
    )
    high = stacked.astype(ml_dtypes.bfloat16)
    low = (stacked - high.astype(np.float64)).astype(ml_dtypes.bfloat16)
    return high, low


def split_high_low(values):
    high = values.astype(jnp.bfloat16)
    low = (values - high.astype(jnp.float32)).astype(jnp.bfloat16)
    return high, low


def dot(left, right):
    return jnp.dot(left, right, preferred_element_type=jnp.float32)


def operator_kernel(
    variable, merged, scalars, slab, field, table_y, high_z, low_z, coef_y, coef_z, own, *rest
):
    if merged:
        out_y, scratch_y, scratch_z = rest
        out_z = None
    else:
        out_y, out_z, scratch_y, scratch_z = rest
    rows, cols = field.shape[1:]
    half_rows = out_y.shape[1]
    half_cols = scratch_z.shape[2]
    stream, sign_y, sign_z = scalars[0], scalars[1], scalars[2]
    fold_y, fold_z = Y_SIGNS[variable], Z_SIGNS[variable]
    u, v, w, p = 0, 2, 4, 6
    base = 2 * variable
    step_y = min(ROW_STEP, half_rows)
    step_z = min(ROW_STEP, rows)
    origin = pl.multiple_of(slab[0] * rows, rows) if merged else 0

    def along_y(part, source, kinds):
        high, low = split_high_low(field[source + part])
        stacked = jnp.concatenate((high, low, high, low), axis=0)
        scratch_y[0 : kinds * half_rows, :] = dot(table_y[0 : kinds * half_rows, :], stacked)

    def along_z(source, kinds):
        both = field[source : source + 2].reshape(2 * rows, cols)
        high, low = split_high_low(both)
        for kind in range(kinds):
            span = slice(kind * half_cols, (kind + 1) * half_cols)
            total = dot(high, high_z[:, span])
            total = total + dot(low, high_z[:, span])
            total = total + dot(high, low_z[:, span])
            scratch_z[kind] = total

    def rows_y(body):
        @pl.loop(0, half_rows // step_y)
        def _(index):
            start = pl.multiple_of(index * step_y, step_y)
            body(start)

    def at(kind, start):
        return scratch_y[pl.ds(kind * half_rows + start, step_y), :]

    for part in (0, 1):
        if variable < 3:
            along_y(part, base, 4)

            def combine(start, part=part):
                span = pl.ds(start, step_y)
                near = coef_y[0, span, :] * at(2, start) + coef_y[1, span, :] * at(0, start)
                far = coef_y[2, span, :] * at(3, start) + coef_y[3, span, :] * at(1, start)
                out_y[part, span, :] = near + fold_y * far

            rows_y(combine)
            if variable == 1:
                along_y(part, p, 2)

                def push(start, part=part):
                    span = pl.ds(start, step_y)
                    out_y[part, span, :] = out_y[part, span, :] - sign_y * (at(0, start) - at(1, start))

                rows_y(push)
        else:
            along_y(part, v, 2)

            def diverge(start, part=part):
                out_y[part, pl.ds(start, step_y), :] = sign_y * (at(0, start) + at(1, start))

            rows_y(diverge)

    def add_z(part, start, values):
        if merged:
            span = pl.ds(origin + start, step_z)
            out_y[part, span, :] = out_y[part, span, :] + values
        else:
            out_z[part, pl.ds(start, step_z), :] = out_z[part, pl.ds(start, step_z), :] + values

    if not merged:
        out_z[...] = jnp.zeros_like(out_z)

    def add_own(part, start, values):
        if merged:
            add_z(part, start, values)
        else:
            span = pl.ds(slab[0] * rows + start, step_z)
            out_y[part, span, :] = out_y[part, span, :] + values

    def rows_z(body):
        @pl.loop(0, rows // step_z)
        def _(index):
            start = pl.multiple_of(index * step_z, step_z)
            for part in (0, 1):
                body(part, start)

    def at_z(kind, part, start):
        return scratch_z[kind, pl.ds(part * rows + start, step_z), :]

    def point(plane, start):
        return field[plane, pl.ds(start, step_z), :]

    turn = (1.0, -1.0)
    if variable < 3:
        along_z(base, 4)

        def combine_z(part, start):
            span = pl.ds(start, step_z)
            near = coef_z[0, span, :] * at_z(2, part, start) + coef_z[1, span, :] * at_z(0, part, start)
            far = coef_z[2, span, :] * at_z(3, part, start) + coef_z[3, span, :] * at_z(1, part, start)
            add_z(part, start, near + fold_z * far)

        def pointwise(part, start):
            span = pl.ds(start, step_z)
            moved = turn[part] * stream * own[0, span, :] * point(base + 1 - part, start)
            made = own[2, span, :] * point(v + part, start) + own[3, span, :] * point(w + part, start)
            lost = own[1, span, :] * (stream * stream) * point(base + part, start)
            values = moved - made - lost
            if variable == 0:
                values = values + turn[part] * stream * point(p + 1 - part, start)
            add_own(part, start, values)

        def both(part, start):
            combine_z(part, start)
            pointwise(part, start)

        rows_z(both)
        if variable == 2:
            along_z(p, 2)

            def push_z(part, start):
                add_z(part, start, -sign_z * (at_z(0, part, start) - at_z(1, part, start)))

            rows_z(push_z)
    else:
        along_z(w, 2)

        def diverge_z(part, start):
            add_z(part, start, sign_z * (at_z(0, part, start) + at_z(1, part, start)))
            add_own(part, start, -turn[part] * stream * point(u + 1 - part, start))

        rows_z(diverge_z)


def apply_variable(variable, merged, half_rows, half_cols, scalars, slab, field, tables, coef_y, coef_z, own):
    rows, cols = field.shape[1:]
    vmem = pl.BlockSpec(memory_space=pltpu.VMEM)
    smem = pl.BlockSpec(memory_space=pltpu.SMEM)
    shapes = [jax.ShapeDtypeStruct((2, half_rows, cols), jnp.float32)]
    if not merged:
        shapes.append(jax.ShapeDtypeStruct((2, rows, half_cols), jnp.float32))
    work = 8 * 2 * (4 * half_rows * 4 * rows * cols + 3 * rows * cols * 4 * half_cols) // 4
    return pl.pallas_call(
        functools.partial(operator_kernel, variable, merged),
        out_shape=tuple(shapes),
        in_specs=[smem, smem] + [vmem] * 7,
        out_specs=tuple(vmem for _ in shapes),
        scratch_shapes=[
            pltpu.VMEM((4 * half_rows, cols), jnp.float32),
            pltpu.VMEM((4, 2 * rows, half_cols), jnp.float32),
        ],
        cost_estimate=pl.CostEstimate(flops=work, bytes_accessed=12 << 20, transcendentals=0),
        name="operator_" + "uvwp"[variable],
    )(scalars, slab, field, *tables, coef_y, coef_z, own)


def mirror_pairs(size):
    return [(i, size - 1 - i) for i in range(size)]


def canonical_pairs(size, bit):
    pairs = []
    for i in range(size):
        if i < size // 2:
            pairs.append((i, i ^ bit))
        else:
            pairs.append((i, size - 1 - ((size - 1 - i) ^ bit)))
    return pairs


def halve(values, axis_name, position, dim):
    size = lax.axis_size(axis_name)
    bit = size // 4
    while bit:
        length = values.shape[dim] // 2
        upper = (position // bit) % 2
        kept = lax.dynamic_slice_in_dim(values, upper * length, length, dim)
        sent = lax.dynamic_slice_in_dim(values, (1 - upper) * length, length, dim)
        values = kept + lax.ppermute(sent, axis_name, canonical_pairs(size, bit))
        bit //= 2
    return values


def gather_coefficients(planes, axis_name, flipped, dim):
    size = lax.axis_size(axis_name)
    gathered = lax.all_gather(planes, axis_name)
    low = jnp.concatenate([gathered[i] for i in range(size // 2)], axis=dim)
    high = jnp.concatenate([gathered[size - 1 - i] for i in range(size // 2)], axis=dim)
    return jnp.where(flipped, high, low), jnp.where(flipped, low, high)


def orient(values, flip_y, flip_z):
    ndim = values.ndim
    return lax.switch(
        2 * flip_y + flip_z,
        [
            lambda x: x,
            lambda x: lax.rev(x, (ndim - 1,)),
            lambda x: lax.rev(x, (ndim - 2,)),
            lambda x: lax.rev(x, (ndim - 2, ndim - 1)),
        ],
        values,
    )


def shards(forcing, wavenumber, mean_flow, viscosity, viscosity_slope):
    vectors, components, rows, cols = forcing.shape
    size_y, size_z = lax.axis_size("gy"), lax.axis_size("gz")
    half_rows, half_cols = rows * size_y // 2, cols * size_z // 2
    index_y, index_z = lax.axis_index("gy"), lax.axis_index("gz")
    flip_y = (index_y >= size_y // 2).astype(jnp.int32)
    flip_z = (index_z >= size_z // 2).astype(jnp.int32)
    place_y = jnp.where(flip_y == 1, size_y - 1 - index_y, index_y)
    place_z = jnp.where(flip_z == 1, size_z - 1 - index_z, index_z)
    sign_y = 1.0 - 2.0 * flip_y.astype(jnp.float32)
    sign_z = 1.0 - 2.0 * flip_z.astype(jnp.float32)
    merged = size_z == 2

    high, low = folded_tables(2 * half_rows)
    slabs = [
        np.concatenate([t[:, s : s + rows] for t in (high, low)], axis=1)
        for s in range(0, half_rows, rows)
    ]
    pair_y = lax.dynamic_index_in_dim(jnp.asarray(np.stack(slabs)), place_y, 0, keepdims=False)
    table_y = jnp.concatenate((pair_y[:, :rows], pair_y[:, :rows], pair_y[:, rows:], pair_y[:, rows:]), axis=1)
    high, low = folded_tables(2 * half_cols)
    slabs = np.stack([np.stack([t[:, s : s + cols].T for t in (high, low)]) for s in range(0, half_cols, cols)])
    if size_z == 2:
        high_z, low_z = jnp.asarray(slabs[0, 0]), jnp.asarray(slabs[0, 1])
    else:
        pair_z = lax.dynamic_index_in_dim(jnp.asarray(slabs), place_z, 0, keepdims=False)
        high_z, low_z = pair_z[0], pair_z[1]
    tables = (table_y, high_z, low_z)

    planes_y = orient(jnp.stack((viscosity, viscosity_slope[0] - mean_flow[1])), flip_y, flip_z)
    near, far = gather_coefficients(planes_y, "gy", flip_y == 1, 1)
    signed = jnp.stack((jnp.float32(1.0), sign_y))[:, None, None]
    coef_y = jnp.concatenate((near * signed, far * signed))
    planes_z = orient(jnp.stack((viscosity, viscosity_slope[1] - mean_flow[2])), flip_y, flip_z)
    near, far = gather_coefficients(planes_z, "gz", flip_z == 1, 2)
    signed = jnp.stack((jnp.float32(1.0), sign_z))[:, None, None]
    coef_z = jnp.concatenate((near * signed, far * signed))
    slopes = orient(jnp.concatenate((mean_flow[0:1], mean_flow[3:9])), flip_y, flip_z)
    own = [
        jnp.stack((slopes[0], planes_y[0], slopes[1 + 2 * c], slopes[2 + 2 * c])) for c in range(3)
    ]
    own.append(own[0])
    scalars = jnp.stack((wavenumber[0], sign_y, sign_z))
    slab = place_y.astype(jnp.int32)[None]

    half = vectors // 2
    chunk = lambda which: 0.25 * orient(
        lax.dynamic_slice_in_dim(forcing, which * half, half, 0), flip_y, flip_z
    )
    sent_field, kept_field = chunk(1 - flip_z), chunk(flip_z)

    def contribution(variable, field):
        parts = []
        for n in range(half):
            got = apply_variable(
                variable, merged, half_rows, half_cols, scalars, slab, field[n], tables, coef_y, coef_z, own[variable]
            )
            if merged:
                parts.append(got[0])
            else:
                full = jnp.zeros((2, half_rows, half_cols), jnp.float32)
                full = lax.dynamic_update_slice_in_dim(full, got[0], place_z * cols, 2)
                start = place_y * rows
                strip = lax.dynamic_slice_in_dim(full, start, rows, 1) + got[1]
                parts.append(lax.dynamic_update_slice_in_dim(full, strip, start, 1))
        total = jnp.concatenate(parts)
        return halve(total, "gz", place_z, 2)

    kept_out, sent_out = [], []
    mirror_y, mirror_z = mirror_pairs(size_y), mirror_pairs(size_z)
    for variable in range(4):
        sent = contribution(variable, sent_field)
        arrived = lax.ppermute(sent, "gz", mirror_z)
        kept = contribution(variable, kept_field) + Z_SIGNS[variable] * arrived
        kept = halve(kept, "gy", place_y, 1)
        kept = kept + Y_SIGNS[variable] * lax.ppermute(kept, "gy", mirror_y)
        back = Z_SIGNS[variable] * lax.ppermute(kept, "gz", mirror_z)
        kept_out.append(kept.reshape(half, 2, rows, cols))
        sent_out.append(back.reshape(half, 2, rows, cols))
    kept = jnp.concatenate(kept_out, axis=1)
    back = jnp.concatenate(sent_out, axis=1)
    first = jnp.where(flip_z == 1, back, kept)
    second = jnp.where(flip_z == 1, kept, back)
    return orient(jnp.concatenate((first, second)), flip_y, flip_z)


def solution(mesh):
    placed = (
        P(("wave", "vec"), None, "gy", "gz"),
        P("wave"),
        P(None, "gy", "gz"),
        P("gy", "gz"),
        P(None, "gy", "gz"),
    )
    return jax.shard_map(
        shards,
        mesh=mesh,
        in_specs=placed,
        out_specs=P(("wave", "vec"), None, "gy", "gz"),
        check_vma=False,
    )
```

```python
import functools
import math

import jax
import jax.numpy as jnp
import ml_dtypes
import numpy as np
from jax import lax
from jax.experimental import pallas as pl
from jax.experimental.pallas import tpu as pltpu
from jax.sharding import PartitionSpec as P


Y_SIGNS = (1.0, -1.0, 1.0, 1.0)
Z_SIGNS = (1.0, 1.0, -1.0, 1.0)
ROW_STEP = 16


def angle_table(points):
    last = points - 1
    row = np.arange(points)[:, None]
    col = np.arange(points)[None, :]
    unit = math.pi / (2.0 * last)
    sine_row = np.sin(2.0 * unit * np.minimum(row, last - row))
    total = row + col
    half_sum = np.sin(unit * np.minimum(total, 2 * last - total))
    half_diff = np.sin(unit * (row - col))
    parity = 1.0 - 2.0 * (total % 2)
    weight = np.where((col == 0) | (col == last), 0.5, 1.0)
    same = row == col
    denominator = np.where(same, 1.0, 2.0 * half_sum * half_diff)
    offdiag = np.where(same, 0.0, math.pi / last * sine_row * parity * weight / denominator)
    return offdiag - np.diag(offdiag.sum(axis=1))


def folded_tables(points):
    table = angle_table(points)
    second = table @ table
    half = points // 2
    stacked = np.concatenate(
        [part for full in (table, second) for part in (full[:half, :half], full[::-1][:half, :half])]
    )
    high = stacked.astype(ml_dtypes.bfloat16)
    low = (stacked - high.astype(np.float64)).astype(ml_dtypes.bfloat16)
    return high, low


def split_high_low(values):
    high = values.astype(jnp.bfloat16)
    low = (values - high.astype(jnp.float32)).astype(jnp.bfloat16)
    return high, low


def dot(left, right):
    return jnp.dot(left, right, preferred_element_type=jnp.float32)


def exchange(size):
    row = lax.broadcasted_iota(jnp.int32, (size, size), 0)
    col = lax.broadcasted_iota(jnp.int32, (size, size), 1)
    return jnp.where(row + col == size - 1, 1.0, 0.0).astype(jnp.bfloat16)


def three_parts(values):
    high = values.astype(jnp.bfloat16)
    rest = values - high.astype(jnp.float32)
    middle = rest.astype(jnp.bfloat16)
    low = (rest - middle.astype(jnp.float32)).astype(jnp.bfloat16)
    return high, middle, low


def store_oriented(flags, planes, out, scale):
    count, rows, cols = planes.shape
    planes = scale * planes

    @pl.when(flags[1] == 0)
    def _():
        out[...] = planes

    @pl.when(flags[1] == 1)
    def _():
        flat = planes.reshape(count * rows, cols)
        matrix = exchange(cols)
        high, middle, low = (dot(part, matrix) for part in three_parts(flat))
        out[...] = ((high + middle) + low).reshape(count, rows, cols)

    @pl.when(flags[0] == 1)
    def _():
        matrix = exchange(rows)
        for n in range(count):
            high, middle, low = (dot(matrix, part) for part in three_parts(out[n]))
            out[n] = (high + middle) + low


def orient_kernel(scale, flags, planes, out):
    store_oriented(flags, planes[...], out, scale)


def orient_planes(values, flags, plane_of, count, group, scale, name):
    rows, cols = values.shape[1:]
    block = (group, rows, cols)
    return pl.pallas_call(
        functools.partial(orient_kernel, scale),
        out_shape=jax.ShapeDtypeStruct((count, rows, cols), jnp.float32),
        grid_spec=pltpu.PrefetchScalarGridSpec(
            num_scalar_prefetch=1,
            grid=(count // group,),
            in_specs=[pl.BlockSpec(block, lambda i, flags: (plane_of(i, flags), 0, 0))],
            out_specs=pl.BlockSpec(block, lambda i, flags: (i, 0, 0)),
        ),
        cost_estimate=pl.CostEstimate(flops=count << 24, bytes_accessed=count << 19, transcendentals=0),
        name=name,
    )(flags, values)


def operator_kernel(variable, merged, shares, spans, scalars, places, *refs):
    refs = list(refs)
    field, table_y, high_z, low_z = refs[:4]
    near_z, far_z, flow, cross_y, cross_z, own_y = refs[4:10]
    taken = 10
    near_y, far_y = [None], []
    for b in range(spans):
        if b:
            near_y.append(refs[taken : taken + shares])
            taken += shares
        far_y.append(refs[taken : taken + shares])
        taken += shares
    taken += 1
    out_y = refs[taken]
    out_z = None if merged else refs[taken + 1]
    scratch_y, scratch_z = refs[-2:]

    rows, cols = field.shape[1:]
    half_rows = out_y.shape[1]
    half_cols = scratch_z.shape[2]
    share_rows = rows // shares
    stream, sign_y, sign_z = scalars[0], scalars[1], scalars[2]
    fold_y, fold_z = Y_SIGNS[variable], Z_SIGNS[variable]
    u, v, w, p = 0, 2, 4, 6
    base = 2 * variable
    step_y = min(ROW_STEP, share_rows)
    step_z = min(ROW_STEP, rows)
    origin = pl.multiple_of(places[0], rows)

    def along_y(part, source, kinds):
        high, low = split_high_low(field[source + part])
        stacked = jnp.concatenate((high, low, high, low), axis=0)
        scratch_y[0 : kinds * half_rows, :] = dot(table_y[0 : kinds * half_rows, :], stacked)

    def along_z(source, kinds):
        both = field[source : source + 2].reshape(2 * rows, cols)
        high, low = split_high_low(both)
        for kind in range(kinds):
            span = slice(kind * half_cols, (kind + 1) * half_cols)
            total = dot(high, high_z[:, span])
            total = total + dot(low, high_z[:, span])
            total = total + dot(high, low_z[:, span])
            scratch_z[kind] = total

    def at(kind, start):
        return scratch_y[pl.ds(kind * half_rows + start, step_y), :]

    def rows_y(body):
        @pl.loop(0, half_rows // step_y)
        def _(index):
            body(pl.multiple_of(index * step_y, step_y))

    for part in (0, 1):
        if variable < 3:
            along_y(part, base, 4)
            for b in range(spans):
                for t in range(shares):
                    offset = pl.multiple_of(places[spans + t], share_rows)
                    first = pl.multiple_of(places[b] + offset, share_rows)

                    @pl.loop(0, share_rows // step_y)
                    def _(index, b=b, t=t, part=part, offset=offset, first=first):
                        inner = pl.multiple_of(index * step_y, step_y)
                        start = pl.multiple_of(first + inner, step_y)
                        local = pl.ds(inner, step_y)
                        if b:
                            viscous, slope = near_y[b][t][0, local, :], near_y[b][t][1, local, :]
                        else:
                            span = pl.ds(pl.multiple_of(offset + inner, step_y), step_y)
                            viscous, slope = own_y[0, span, :], own_y[1, span, :]
                        near = viscous * at(2, start) + slope * at(0, start)
                        far = far_y[b][t][0, local, :] * at(3, start) - far_y[b][t][1, local, :] * at(1, start)
                        out_y[part, pl.ds(start, step_y), :] = near + fold_y * far

            if variable == 1:
                along_y(part, p, 2)

                def push(start, part=part):
                    span = pl.ds(start, step_y)
                    out_y[part, span, :] = out_y[part, span, :] - sign_y * (at(0, start) - at(1, start))

                rows_y(push)
        else:
            along_y(part, v, 2)

            def diverge(start, part=part):
                out_y[part, pl.ds(start, step_y), :] = sign_y * (at(0, start) + at(1, start))

            rows_y(diverge)

    def add_own(part, start, values):
        span = pl.ds(pl.multiple_of(origin + start, step_z), step_z)
        out_y[part, span, :] = out_y[part, span, :] + values

    def add_z(part, start, values):
        if merged:
            add_own(part, start, values)
        else:
            span = pl.ds(start, step_z)
            out_z[part, span, :] = out_z[part, span, :] + values

    if not merged:
        out_z[...] = jnp.zeros_like(out_z)

    def rows_z(body):
        @pl.loop(0, rows // step_z)
        def _(index):
            start = pl.multiple_of(index * step_z, step_z)
            for part in (0, 1):
                body(part, start)

    def at_z(kind, part, start):
        return scratch_z[kind, pl.ds(part * rows + start, step_z), :]

    def point(plane, start):
        return field[plane, pl.ds(start, step_z), :]

    turn = (1.0, -1.0)
    if variable < 3:
        along_z(base, 4)

        def both(part, start):
            span = pl.ds(start, step_z)
            near = near_z[0, span, :] * at_z(2, part, start) + near_z[1, span, :] * at_z(0, part, start)
            far = far_z[0, span, :] * at_z(3, part, start) - far_z[1, span, :] * at_z(1, part, start)
            add_z(part, start, near + fold_z * far)
            moved = turn[part] * stream * flow[0, span, :] * point(base + 1 - part, start)
            made = cross_y[0, span, :] * point(v + part, start) + cross_z[0, span, :] * point(w + part, start)
            lost = own_y[0, span, :] * (stream * stream) * point(base + part, start)
            values = moved - made - lost
            if variable == 0:
                values = values + turn[part] * stream * point(p + 1 - part, start)
            add_own(part, start, values)

        rows_z(both)
        if variable == 2:
            along_z(p, 2)

            def push_z(part, start):
                add_z(part, start, -sign_z * (at_z(0, part, start) - at_z(1, part, start)))

            rows_z(push_z)
    else:
        along_z(w, 2)

        def diverge_z(part, start):
            add_z(part, start, sign_z * (at_z(0, part, start) + at_z(1, part, start)))
            add_own(part, start, -turn[part] * stream * point(u + 1 - part, start))

        rows_z(diverge_z)


def whole(shape):
    return pl.BlockSpec(shape, lambda i: (0,) * len(shape), pipeline_mode=pl.Buffered(1))


def apply_variable(variable, merged, shares, half_cols, scalars, places, field, tables, coefs, token):
    near_z, far_z, flows, own_y, pieces = coefs
    rows, cols = field.shape[1:]
    half_rows = tables[0].shape[0] // 4
    spans = half_rows // rows
    plane = min(variable, 2)
    pick = lambda k: pl.BlockSpec((1, rows, cols), lambda i: (k, 0, 0), pipeline_mode=pl.Buffered(1))
    smem = pl.BlockSpec(memory_space=pltpu.SMEM)
    shapes = [jax.ShapeDtypeStruct((2, half_rows, cols), jnp.float32)]
    if not merged:
        shapes.append(jax.ShapeDtypeStruct((2, rows, half_cols), jnp.float32))
    arrays = [field, *tables, near_z, far_z]
    specs = [whole(a.shape) for a in arrays]
    specs += [pick(0), pick(1 + 2 * plane), pick(2 + 2 * plane)]
    arrays += [flows, flows, flows, own_y, *pieces]
    specs += [whole(a.shape) for a in (own_y, *pieces)]
    arrays.append(token)
    specs.append(pl.BlockSpec(memory_space=pl.ANY))
    work = 8 * 2 * (4 * half_rows * 4 * rows * cols + 3 * rows * cols * 4 * half_cols) // 4
    return pl.pallas_call(
        functools.partial(operator_kernel, variable, merged, shares, spans),
        out_shape=tuple(shapes),
        grid=(1,),
        in_specs=[smem, smem] + specs,
        out_specs=tuple(whole(s.shape) for s in shapes),
        scratch_shapes=[
            pltpu.VMEM((4 * half_rows, cols), jnp.float32),
            pltpu.VMEM((4, 2 * rows, half_cols), jnp.float32),
        ],
        cost_estimate=pl.CostEstimate(flops=work, bytes_accessed=12 << 20, transcendentals=0),
        name="operator_" + "uvwp"[variable],
    )(scalars, places, *arrays)


def fold_kernel(sign, places, mine, theirs, token, kept, sent):
    rows = kept.shape[1]
    for part in range(mine.shape[0]):
        for slab, out in ((0, kept), (1, sent)):
            span = pl.ds(pl.multiple_of(places[slab], rows), rows)
            out[part] = mine[part, span, :] + sign * theirs[part, span, :]


def add_kernel(sign, mine, theirs, token, out):
    out[...] = mine[...] + sign * theirs[...]


def small_call(kernel, out_shapes, arrays, token, name, scalars=()):
    vmem = pl.BlockSpec(memory_space=pltpu.VMEM)
    smem = pl.BlockSpec(memory_space=pltpu.SMEM)
    return pl.pallas_call(
        kernel,
        out_shape=tuple(jax.ShapeDtypeStruct(s, jnp.float32) for s in out_shapes),
        in_specs=[smem] * len(scalars) + [vmem] * len(arrays) + [pl.BlockSpec(memory_space=pl.ANY)],
        out_specs=tuple(vmem for _ in out_shapes),
        cost_estimate=pl.CostEstimate(flops=1 << 20, bytes_accessed=3 << 20, transcendentals=0),
        name=name,
    )(*scalars, *arrays, token)


def finish_kernel(sign, flags, kept, back, *rest):
    out = rest[-1]
    block = out.at[0]

    @pl.when(pl.program_id(0) == flags[1])
    def _():
        store_oriented(flags, kept[...], block, 1.0)

    @pl.when(pl.program_id(0) != flags[1])
    def _():
        store_oriented(flags, back[...], block, sign)


def finish(variable, flags, kept, back, response, token):
    parts, rows, cols = kept.shape
    shape = (2, 8, rows, cols)
    anywhere = pl.BlockSpec(memory_space=pl.ANY)
    spec = pl.BlockSpec((parts, rows, cols), lambda i, flags: (0, 0, 0), pipeline_mode=pl.Buffered(1))
    arrays = [kept, back]
    if response is None or token is not response:
        arrays.append(token)
    if response is not None:
        arrays.append(response)
    return pl.pallas_call(
        functools.partial(finish_kernel, Z_SIGNS[variable]),
        out_shape=jax.ShapeDtypeStruct(shape, jnp.float32),
        grid_spec=pltpu.PrefetchScalarGridSpec(
            num_scalar_prefetch=1,
            grid=(2,),
            in_specs=[spec, spec] + [anywhere] * (len(arrays) - 2),
            out_specs=pl.BlockSpec((1, parts, rows, cols), lambda i, flags: (i, variable, 0, 0)),
        ),
        input_output_aliases={} if response is None else {len(arrays): 0},
        cost_estimate=pl.CostEstimate(flops=1 << 26, bytes_accessed=2 << 20, transcendentals=0),
        name="finish_" + "uvwp"[variable],
    )(flags, *arrays)


def partner_pairs(size, bit, mirrored):
    pairs = []
    for i in range(size):
        far_end = i >= size // 2
        place = (size - 1 - i if far_end else i) ^ bit
        pairs.append((i, size - 1 - place if far_end != mirrored else place))
    return pairs


def halve(values, axis_name, position, dim):
    size = lax.axis_size(axis_name)
    bit = size // 4
    while bit:
        length = values.shape[dim] // 2
        upper = (position // bit) % 2
        kept = lax.dynamic_slice_in_dim(values, upper * length, length, dim)
        sent = lax.dynamic_slice_in_dim(values, (1 - upper) * length, length, dim)
        values = kept + lax.ppermute(sent, axis_name, partner_pairs(size, bit, False))
        bit //= 2
    return values


def gather_coefficients(planes, axis_name, flipped, dim):
    size = lax.axis_size(axis_name)
    gathered = lax.all_gather(planes, axis_name)
    low = jnp.concatenate([gathered[i] for i in range(size // 2)], axis=dim)
    high = jnp.concatenate([gathered[size - 1 - i] for i in range(size // 2)], axis=dim)
    return jnp.where(flipped, high, low), jnp.where(flipped, low, high)


def shards(forcing, wavenumber, mean_flow, viscosity, viscosity_slope):
    vectors, components, rows, cols = forcing.shape
    size_y, size_z, size_v = lax.axis_size("gy"), lax.axis_size("gz"), lax.axis_size("vec")
    half_rows, half_cols = rows * size_y // 2, cols * size_z // 2
    index_y, index_z = lax.axis_index("gy"), lax.axis_index("gz")
    flip_y = (index_y >= size_y // 2).astype(jnp.int32)
    flip_z = (index_z >= size_z // 2).astype(jnp.int32)
    place_y = jnp.where(flip_y == 1, size_y - 1 - index_y, index_y).astype(jnp.int32)
    place_z = jnp.where(flip_z == 1, size_z - 1 - index_z, index_z).astype(jnp.int32)
    sign_y = 1.0 - 2.0 * flip_y.astype(jnp.float32)
    sign_z = 1.0 - 2.0 * flip_z.astype(jnp.float32)
    flags = jnp.stack((flip_y, flip_z))
    merged = size_z == 2
    spans = size_y // 2
    half = vectors // 2

    near_planes = orient_planes(
        jnp.stack(
            (
                viscosity,
                sign_y * (viscosity_slope[0] - mean_flow[1]),
                sign_z * (viscosity_slope[1] - mean_flow[2]),
            )
        ),
        flags, lambda i, flags: 0, 3, 3, 1.0, "orient_planes",
    )
    own_y, own_z = near_planes[0:2], near_planes[0:3:2]
    shares = size_v if rows % (8 * size_v) == 0 else 1
    share_rows = rows // shares
    share = lax.axis_index("vec").astype(jnp.int32) if shares > 1 else jnp.int32(0)
    sent = lax.dynamic_slice_in_dim(own_y, share * share_rows, share_rows, 1)
    turn = [[(i, (i + k) % shares) for i in range(shares)] for k in range(shares)]
    pieces = []
    for b in range(spans):
        for mirrored in (False, True):
            if not b and not mirrored:
                continue
            got = lax.ppermute(sent, "gy", partner_pairs(size_y, b, mirrored))
            pieces += [got] + [lax.ppermute(got, "vec", turn[k]) for k in range(1, shares)]
    places = jnp.stack(
        [(place_y ^ b) * rows for b in range(spans)]
        + [((share - k) % shares) * share_rows for k in range(shares)]
    )
    if merged:
        near_z, far_z = own_z, lax.ppermute(own_z, "gz", partner_pairs(size_z, 0, True))
    else:
        near_z, far_z = gather_coefficients(own_z, "gz", flip_z == 1, 2)
    flows = orient_planes(
        mean_flow, flags, lambda i, flags: jnp.where(i == 0, 0, i + 2), 7, 1, 1.0, "orient_flow"
    )
    scalars = jnp.stack((wavenumber[0], sign_y, sign_z))
    coefs = (near_z, far_z, flows, own_y, pieces)

    high, low = folded_tables(2 * half_rows)
    slabs = [
        np.concatenate([t[:, s : s + rows] for t in (high, low)], axis=1)
        for s in range(0, half_rows, rows)
    ]
    pair_y = lax.dynamic_index_in_dim(jnp.asarray(np.stack(slabs)), place_y, 0, keepdims=False)
    table_y = jnp.concatenate((pair_y[:, :rows], pair_y[:, :rows], pair_y[:, rows:], pair_y[:, rows:]), axis=1)
    high, low = folded_tables(2 * half_cols)
    slabs = np.stack([np.stack([t[:, s : s + cols].T for t in (high, low)]) for s in range(0, half_cols, cols)])
    if size_z == 2:
        high_z, low_z = jnp.asarray(slabs[0, 0]), jnp.asarray(slabs[0, 1])
    else:
        pair_z = lax.dynamic_index_in_dim(jnp.asarray(slabs), place_z, 0, keepdims=False)
        high_z, low_z = pair_z[0], pair_z[1]
    tables = (table_y, high_z, low_z)

    planes = forcing.reshape(vectors * components, rows, cols)
    count = half * components
    group = 4

    def oriented(other):
        def plane_of(i, flags):
            which = 1 - flags[1] if other else flags[1]
            return which * (count // group) + i

        return orient_planes(planes, flags, plane_of, count, group, 0.25, "orient_field")

    sent_field, kept_field = oriented(True), oriented(False)

    def apply(variable, field, token):
        return apply_variable(variable, merged, shares, half_cols, scalars, places, field, tables, coefs, token)

    mirror_y, mirror_z = partner_pairs(size_y, 0, True), partner_pairs(size_z, 0, True)
    if merged and size_y == 4 and half == 1:
        return pipeline(apply, sent_field, kept_field, places, flags, mirror_y, mirror_z)

    def contribution(variable, field):
        parts = []
        for n in range(half):
            got = apply(variable, field[n * components : (n + 1) * components], scalars)
            if merged:
                parts.append(got[0])
            else:
                full = jnp.zeros((2, half_rows, half_cols), jnp.float32)
                full = lax.dynamic_update_slice_in_dim(full, got[0], place_z * cols, 2)
                start = place_y * rows
                strip = lax.dynamic_slice_in_dim(full, start, rows, 1) + got[1]
                parts.append(lax.dynamic_update_slice_in_dim(full, strip, start, 1))
        return halve(jnp.concatenate(parts), "gz", place_z, 2)

    kept_out, sent_out = [], []
    for variable in range(4):
        arrived = lax.ppermute(contribution(variable, sent_field), "gz", mirror_z)
        kept = contribution(variable, kept_field) + Z_SIGNS[variable] * arrived
        kept = halve(kept, "gy", place_y, 1)
        kept = kept + Y_SIGNS[variable] * lax.ppermute(kept, "gy", mirror_y)
        back = Z_SIGNS[variable] * lax.ppermute(kept, "gz", mirror_z)
        kept_out.append(kept.reshape(half, 2, rows, cols))
        sent_out.append(back.reshape(half, 2, rows, cols))
    kept = jnp.concatenate(kept_out, axis=1)
    back = jnp.concatenate(sent_out, axis=1)
    first = jnp.where(flip_z == 1, back, kept)
    second = jnp.where(flip_z == 1, kept, back)
    both = jnp.concatenate((first, second)).reshape(vectors * components, rows, cols)
    out = orient_planes(both, flags, lambda i, flags: i, vectors * components, group, 1.0, "orient_response")
    return out.reshape(forcing.shape)


def pipeline(apply, sent_field, kept_field, places, flags, mirror_y, mirror_z):
    rows, cols = sent_field.shape[1:]
    neighbour_y = partner_pairs(4, 1, False)
    token = places
    small = (2, rows, cols)
    state = [dict() for _ in range(4)]
    response = None

    def send(n):
        nonlocal token
        token = apply(n, sent_field, token)[0]
        state[n]["x"] = lax.ppermute(token, "gz", mirror_z)

    def keep(n):
        nonlocal token
        state[n]["kept"] = token = apply(n, kept_field, token)[0]

    def fold_x(n):
        nonlocal token
        s = state[n]
        s["kept"], token = small_call(
            functools.partial(fold_kernel, Z_SIGNS[n]), (small, small), (s["kept"], s["x"]), token, "fold_x", (places,)
        )
        s["y"] = lax.ppermute(token, "gy", neighbour_y)

    def fold_y(n):
        nonlocal token
        s = state[n]
        s["kept"] = token = small_call(
            functools.partial(add_kernel, 1.0), (small,), (s["kept"], s["y"]), token, "fold_y"
        )[0]
        s["m"] = lax.ppermute(token, "gy", mirror_y)

    def fold_m(n):
        nonlocal token
        s = state[n]
        s["kept"] = token = small_call(
            functools.partial(add_kernel, Y_SIGNS[n]), (small,), (s["kept"], s["m"]), token, "fold_m"
        )[0]
        s["back"] = lax.ppermute(token, "gz", mirror_z)

    def write(n):
        nonlocal token, response
        response = token = finish(n, flags, state[n]["kept"], state[n]["back"], response, token)

    for step, n in ORDER:
        {"S": send, "K": keep, "X": fold_x, "Y": fold_y, "M": fold_m, "W": write}[step](n)
    return response


ORDER = [
    (step[0], "uvwp".index(step[1]))
    for step in "Su Sv Ku Xu Sw Yu Kv Xv Sp Mu Yv Kw Xw Kp Mv Yw Xp Wu Mw Yp Wv Mp Ww Wp".split()
]


def solution(mesh):
    placed = (
        P(("wave", "vec"), None, "gy", "gz"),
        P("wave"),
        P(None, "gy", "gz"),
        P("gy", "gz"),
        P(None, "gy", "gz"),
    )
    return jax.shard_map(
        shards,
        mesh=mesh,
        in_specs=placed,
        out_specs=P(("wave", "vec"), None, "gy", "gz"),
        check_vma=False,
    )
```

```python
import functools
import math

import jax
import jax.numpy as jnp
import ml_dtypes
import numpy as np
from jax import lax
from jax.experimental import pallas as pl
from jax.experimental.pallas import tpu as pltpu
from jax.sharding import PartitionSpec as P


Y_SIGNS = (1.0, -1.0, 1.0, 1.0)
Z_SIGNS = (1.0, 1.0, -1.0, 1.0)
ROW_STEP = 16


def angle_table(points):
    last = points - 1
    row = np.arange(points)[:, None]
    col = np.arange(points)[None, :]
    unit = math.pi / (2.0 * last)
    sine_row = np.sin(2.0 * unit * np.minimum(row, last - row))
    total = row + col
    half_sum = np.sin(unit * np.minimum(total, 2 * last - total))
    half_diff = np.sin(unit * (row - col))
    parity = 1.0 - 2.0 * (total % 2)
    weight = np.where((col == 0) | (col == last), 0.5, 1.0)
    same = row == col
    denominator = np.where(same, 1.0, 2.0 * half_sum * half_diff)
    offdiag = np.where(same, 0.0, math.pi / last * sine_row * parity * weight / denominator)
    return offdiag - np.diag(offdiag.sum(axis=1))


def folded_tables(points):
    table = angle_table(points)
    second = table @ table
    half = points // 2
    stacked = np.concatenate(
        [part for full in (table, second) for part in (full[:half, :half], full[::-1][:half, :half])]
    )
    high = stacked.astype(ml_dtypes.bfloat16)
    low = (stacked - high.astype(np.float64)).astype(ml_dtypes.bfloat16)
    return high, low


def split_high_low(values):
    high = values.astype(jnp.bfloat16)
    low = (values - high.astype(jnp.float32)).astype(jnp.bfloat16)
    return high, low


def dot(left, right):
    return jnp.dot(left, right, preferred_element_type=jnp.float32)


def in_vmem(values):
    return pltpu.with_memory_space_constraint(values, pltpu.VMEM)


def vmem_result(shape):
    return pltpu.VMEM(shape, jnp.float32)


def exchange(size):
    row = lax.broadcasted_iota(jnp.int32, (size, size), 0)
    col = lax.broadcasted_iota(jnp.int32, (size, size), 1)
    return jnp.where(row + col == size - 1, 1.0, 0.0).astype(jnp.bfloat16)


def three_parts(values):
    high = values.astype(jnp.bfloat16)
    rest = values - high.astype(jnp.float32)
    middle = rest.astype(jnp.bfloat16)
    low = (rest - middle.astype(jnp.float32)).astype(jnp.bfloat16)
    return high, middle, low


def store_oriented(flags, planes, out, scale):
    count, rows, cols = planes.shape
    planes = scale * planes

    @pl.when(flags[1] == 0)
    def _():
        out[...] = planes

    @pl.when(flags[1] == 1)
    def _():
        flat = planes.reshape(count * rows, cols)
        matrix = exchange(cols)
        high, middle, low = (dot(part, matrix) for part in three_parts(flat))
        out[...] = ((high + middle) + low).reshape(count, rows, cols)

    @pl.when(flags[0] == 1)
    def _():
        matrix = exchange(rows)
        for n in range(count):
            high, middle, low = (dot(matrix, part) for part in three_parts(out[n]))
            out[n] = (high + middle) + low


def orient_kernel(scale, picks, flags, values, token, out, planes, sems):
    copies = []
    for n, (source, count, place) in enumerate(picks(flags)):
        copies.append(
            pltpu.make_async_copy(values.at[pl.ds(source, count)], planes.at[pl.ds(place, count)], sems.at[n])
        )
    for copy in copies:
        copy.start()
    for copy in copies:
        copy.wait()
    store_oriented(flags, planes[...], out, scale)


def orient_planes(values, flags, picks, runs, count, scale, token, name):
    shape = (count,) + values.shape[1:]
    anywhere = pl.BlockSpec(memory_space=pl.ANY)
    return pl.pallas_call(
        functools.partial(orient_kernel, scale, picks),
        out_shape=vmem_result(shape),
        in_specs=[pl.BlockSpec(memory_space=pltpu.SMEM), anywhere, anywhere],
        out_specs=pl.BlockSpec(memory_space=pltpu.VMEM),
        scratch_shapes=[pltpu.VMEM(shape, jnp.float32), pltpu.SemaphoreType.DMA((runs,))],
        compiler_params=pltpu.CompilerParams(vmem_limit_bytes=28 << 20),
        cost_estimate=pl.CostEstimate(flops=count << 24, bytes_accessed=count << 19, transcendentals=0),
        name=name,
    )(flags, values, token)


def prepare_kernel(flags, signs, share, flow, viscosity, slope, own_y, own_z, sent, work, oriented, sems):
    copies = (
        pltpu.make_async_copy(viscosity, work.at[0], sems.at[0]),
        pltpu.make_async_copy(slope, work.at[pl.ds(1, 2)], sems.at[1]),
        pltpu.make_async_copy(flow.at[pl.ds(1, 2)], work.at[pl.ds(3, 2)], sems.at[2]),
    )
    for copy in copies:
        copy.start()
    for copy in copies:
        copy.wait()
    for n in (1, 2):
        work[n] = signs[n] * (work[n] - work[n + 2])
    store_oriented(flags, work[0:3], oriented, 1.0)
    own_y[...] = oriented[0:2]
    own_z[0] = oriented[0]
    own_z[1] = oriented[2]
    rows = sent.shape[1]
    span = pl.ds(pl.multiple_of(share[0] * rows, rows), rows)
    for n in (0, 1):
        sent[n] = oriented[n, span, :]


def prepare(flags, signs, share, share_rows, flow, viscosity, slope):
    rows, cols = viscosity.shape
    smem, anywhere = pl.BlockSpec(memory_space=pltpu.SMEM), pl.BlockSpec(memory_space=pl.ANY)
    shapes = ((2, rows, cols), (2, rows, cols), (2, share_rows, cols))
    return pl.pallas_call(
        prepare_kernel,
        out_shape=tuple(vmem_result(s) for s in shapes),
        in_specs=[smem] * 3 + [anywhere] * 3,
        out_specs=(pl.BlockSpec(memory_space=pltpu.VMEM),) * 3,
        scratch_shapes=[
            pltpu.VMEM((5, rows, cols), jnp.float32),
            pltpu.VMEM((3, rows, cols), jnp.float32),
            pltpu.SemaphoreType.DMA((3,)),
        ],
        compiler_params=pltpu.CompilerParams(vmem_limit_bytes=28 << 20),
        cost_estimate=pl.CostEstimate(flops=1 << 26, bytes_accessed=3 << 20, transcendentals=0),
        name="prepare",
    )(flags, signs, share, flow, viscosity, slope)


def operator_kernel(variable, merged, split, shares, spans, scalars, places, *refs):
    refs = list(refs)
    field, table_y, high_z, low_z = refs[:4]
    near_z, far_z, flows, own_y = refs[4:8]
    taken = 8
    plane = min(variable, 2)
    near_y, far_y = [None], []
    for b in range(spans):
        if b:
            near_y.append(refs[taken : taken + shares])
            taken += shares
        far_y.append(refs[taken : taken + shares])
        taken += shares
    taken += 1
    outs_y = [refs[taken].at[0], refs[taken + 1].at[0]] if split else [refs[taken].at[n] for n in (0, 1)]
    out_z = None if merged else refs[taken + 1]
    scratch_y, scratch_z = refs[-2:]

    rows, cols = field.shape[1:]
    half_rows = outs_y[0].shape[0]
    half_cols = scratch_z.shape[2]
    share_rows = rows // shares
    stream, sign_y, sign_z = scalars[0], scalars[1], scalars[2]
    fold_y, fold_z = Y_SIGNS[variable], Z_SIGNS[variable]
    u, v, w, p = 0, 2, 4, 6
    base = 2 * variable
    step_y = min(ROW_STEP, share_rows)
    step_z = min(ROW_STEP, rows)
    origin = pl.multiple_of(places[0], rows)

    def along_y(part, source, kinds):
        high, low = split_high_low(field[source + part])
        stacked = jnp.concatenate((high, low, high, low), axis=0)
        scratch_y[0 : kinds * half_rows, :] = dot(table_y[0 : kinds * half_rows, :], stacked)

    def along_z(source, kinds):
        both = field[source : source + 2].reshape(2 * rows, cols)
        high, low = split_high_low(both)
        for kind in range(kinds):
            span = slice(kind * half_cols, (kind + 1) * half_cols)
            total = dot(high, high_z[:, span])
            total = total + dot(low, high_z[:, span])
            total = total + dot(high, low_z[:, span])
            scratch_z[kind] = total

    def at(kind, start):
        return scratch_y[pl.ds(kind * half_rows + start, step_y), :]

    def rows_y(body):
        @pl.loop(0, half_rows // step_y)
        def _(index):
            body(pl.multiple_of(index * step_y, step_y))

    for part in (0, 1):
        if variable < 3:
            along_y(part, base, 4)
            for b in range(spans):
                for t in range(shares):
                    offset = pl.multiple_of(places[spans + t], share_rows)
                    first = pl.multiple_of(places[b] + offset, share_rows)

                    @pl.loop(0, share_rows // step_y)
                    def _(index, b=b, t=t, part=part, offset=offset, first=first):
                        inner = pl.multiple_of(index * step_y, step_y)
                        start = pl.multiple_of(first + inner, step_y)
                        local = pl.ds(inner, step_y)
                        if b:
                            viscous, slope = near_y[b][t][0, local, :], near_y[b][t][1, local, :]
                        else:
                            span = pl.ds(pl.multiple_of(offset + inner, step_y), step_y)
                            viscous, slope = own_y[0, span, :], own_y[1, span, :]
                        near = viscous * at(2, start) + slope * at(0, start)
                        far = far_y[b][t][0, local, :] * at(3, start) - far_y[b][t][1, local, :] * at(1, start)
                        outs_y[part][pl.ds(start, step_y), :] = near + fold_y * far

            if variable == 1:
                along_y(part, p, 2)

                def push(start, part=part):
                    span = pl.ds(start, step_y)
                    outs_y[part][span, :] = outs_y[part][span, :] - sign_y * (at(0, start) - at(1, start))

                rows_y(push)
        else:
            along_y(part, v, 2)

            def diverge(start, part=part):
                outs_y[part][pl.ds(start, step_y), :] = sign_y * (at(0, start) + at(1, start))

            rows_y(diverge)

    def add_own(part, start, values):
        span = pl.ds(pl.multiple_of(origin + start, step_z), step_z)
        outs_y[part][span, :] = outs_y[part][span, :] + values

    def add_z(part, start, values):
        if merged:
            add_own(part, start, values)
        else:
            span = pl.ds(start, step_z)
            out_z[part, span, :] = out_z[part, span, :] + values

    if not merged:
        out_z[...] = jnp.zeros_like(out_z)

    def rows_z(body):
        @pl.loop(0, rows // step_z)
        def _(index):
            start = pl.multiple_of(index * step_z, step_z)
            for part in (0, 1):
                body(part, start)

    def at_z(kind, part, start):
        return scratch_z[kind, pl.ds(part * rows + start, step_z), :]

    def point(plane, start):
        return field[plane, pl.ds(start, step_z), :]

    turn = (1.0, -1.0)
    if variable < 3:
        along_z(base, 4)

        def both(part, start):
            span = pl.ds(start, step_z)
            near = near_z[0, span, :] * at_z(2, part, start) + near_z[1, span, :] * at_z(0, part, start)
            far = far_z[0, span, :] * at_z(3, part, start) - far_z[1, span, :] * at_z(1, part, start)
            add_z(part, start, near + fold_z * far)
            moved = turn[part] * stream * flows[0, span, :] * point(base + 1 - part, start)
            made = flows[1 + 2 * plane, span, :] * point(v + part, start) + flows[2 + 2 * plane, span, :] * point(w + part, start)
            lost = own_y[0, span, :] * (stream * stream) * point(base + part, start)
            values = moved - made - lost
            if variable == 0:
                values = values + turn[part] * stream * point(p + 1 - part, start)
            add_own(part, start, values)

        rows_z(both)
        if variable == 2:
            along_z(p, 2)

            def push_z(part, start):
                add_z(part, start, -sign_z * (at_z(0, part, start) - at_z(1, part, start)))

            rows_z(push_z)
    else:
        along_z(w, 2)

        def diverge_z(part, start):
            add_z(part, start, sign_z * (at_z(0, part, start) + at_z(1, part, start)))
            add_own(part, start, -turn[part] * stream * point(u + 1 - part, start))

        rows_z(diverge_z)


def call_in_vmem(kernel, out_shapes, scalars, arrays, token, name, flops, scratch=(), limit=16):
    vmem = pl.BlockSpec(memory_space=pltpu.VMEM)
    smem = pl.BlockSpec(memory_space=pltpu.SMEM)
    return pl.pallas_call(
        kernel,
        out_shape=tuple(vmem_result(s) for s in out_shapes),
        in_specs=[smem] * len(scalars) + [vmem] * len(arrays) + [pl.BlockSpec(memory_space=pl.ANY)],
        out_specs=tuple(vmem for _ in out_shapes),
        scratch_shapes=list(scratch),
        compiler_params=pltpu.CompilerParams(vmem_limit_bytes=limit << 20),
        cost_estimate=pl.CostEstimate(flops=flops, bytes_accessed=3 << 20, transcendentals=0),
        name=name,
    )(*scalars, *(in_vmem(a) for a in arrays), token)


def apply_variable(variable, merged, split, shares, half_cols, scalars, places, field, tables, coefs, token):
    near_z, far_z, flows, own_y, pieces = coefs
    rows, cols = field.shape[1:]
    half_rows = tables[0].shape[0] // 4
    spans = half_rows // rows
    shapes = [(1, half_rows, cols)] * 2 if split else [(2, half_rows, cols)]
    if not merged:
        shapes.append((2, rows, half_cols))
    work = 8 * 2 * (4 * half_rows * 4 * rows * cols + 3 * rows * cols * 4 * half_cols) // 4
    return call_in_vmem(
        functools.partial(operator_kernel, variable, merged, split, shares, spans),
        shapes,
        (scalars, places),
        (field, *tables, near_z, far_z, flows, own_y, *pieces),
        token,
        "operator_" + "uvwp"[variable],
        work,
        (
            pltpu.VMEM((4 * half_rows, cols), jnp.float32),
            pltpu.VMEM((4, 2 * rows, half_cols), jnp.float32),
        ),
        28,
    )


def fold_kernel(sign, places, mine, theirs, token, kept, sent):
    rows = kept.shape[1]
    for part in range(mine.shape[0]):
        for slab, out in ((0, kept), (1, sent)):
            span = pl.ds(pl.multiple_of(places[slab], rows), rows)
            out[part] = mine[part, span, :] + sign * theirs[part, span, :]


def add_kernel(sign, mine, theirs, token, out):
    out[...] = mine[...] + sign * theirs[...]


def small_call(kernel, out_shapes, arrays, token, name, scalars=()):
    return call_in_vmem(kernel, out_shapes, scalars, arrays, token, name, 1 << 20)


def finish_kernel(sign, count, first, flags, *refs):
    kept, back, out, staged, sems = refs[:count], refs[count : 2 * count], refs[-3], refs[-2], refs[-1]
    for vector, (sources, factor) in enumerate(((kept, 1.0), (back, sign))):
        place = flags[1] if vector == 0 else 1 - flags[1]
        values = jnp.concatenate([ref[...] for ref in sources]) if count > 1 else sources[0][...]
        store_oriented(flags, values, staged.at[vector], factor)
        pltpu.make_async_copy(
            staged.at[vector], out.at[place, pl.ds(first, 2)], sems.at[vector]
        ).start()
    for vector in (0, 1):
        place = flags[1] if vector == 0 else 1 - flags[1]
        pltpu.make_async_copy(
            staged.at[vector], out.at[place, pl.ds(first, 2)], sems.at[vector]
        ).wait()


def finish(variable, flags, kept, back, response, token):
    rows, cols = kept[0].shape[1:]
    anywhere, vmem = pl.BlockSpec(memory_space=pl.ANY), pl.BlockSpec(memory_space=pltpu.VMEM)
    count = len(kept)
    arrays = [in_vmem(a) for a in (*kept, *back)]
    specs = [pl.BlockSpec(memory_space=pltpu.SMEM)] + [vmem] * len(arrays)
    extras = [token] if response is None else [response] if token is response else [token, response]
    arrays += extras
    specs += [anywhere] * len(extras)
    return pl.pallas_call(
        functools.partial(finish_kernel, Z_SIGNS[variable], count, 2 * variable),
        out_shape=jax.ShapeDtypeStruct((2, 8, rows, cols), jnp.float32),
        in_specs=specs,
        out_specs=anywhere,
        scratch_shapes=[pltpu.VMEM((2, 2, rows, cols), jnp.float32), pltpu.SemaphoreType.DMA((2,))],
        input_output_aliases={} if response is None else {len(arrays): 0},
        compiler_params=pltpu.CompilerParams(vmem_limit_bytes=16 << 20),
        cost_estimate=pl.CostEstimate(flops=1 << 26, bytes_accessed=2 << 20, transcendentals=0),
        name="finish_" + "uvwp"[variable],
    )(flags, *arrays)


def partner_pairs(size, bit, mirrored):
    pairs = []
    for i in range(size):
        far_end = i >= size // 2
        place = (size - 1 - i if far_end else i) ^ bit
        pairs.append((i, size - 1 - place if far_end != mirrored else place))
    return pairs


def halve(values, axis_name, position, dim):
    size = lax.axis_size(axis_name)
    bit = size // 4
    while bit:
        length = values.shape[dim] // 2
        upper = (position // bit) % 2
        kept = lax.dynamic_slice_in_dim(values, upper * length, length, dim)
        sent = lax.dynamic_slice_in_dim(values, (1 - upper) * length, length, dim)
        values = kept + lax.ppermute(sent, axis_name, partner_pairs(size, bit, False))
        bit //= 2
    return values


def gather_coefficients(planes, axis_name, flipped, dim):
    size = lax.axis_size(axis_name)
    gathered = lax.all_gather(planes, axis_name)
    low = jnp.concatenate([gathered[i] for i in range(size // 2)], axis=dim)
    high = jnp.concatenate([gathered[size - 1 - i] for i in range(size // 2)], axis=dim)
    return jnp.where(flipped, high, low), jnp.where(flipped, low, high)


def shards(forcing, wavenumber, mean_flow, viscosity, viscosity_slope):
    vectors, components, rows, cols = forcing.shape
    size_y, size_z, size_v = lax.axis_size("gy"), lax.axis_size("gz"), lax.axis_size("vec")
    half_rows, half_cols = rows * size_y // 2, cols * size_z // 2
    index_y, index_z = lax.axis_index("gy"), lax.axis_index("gz")
    flip_y = (index_y >= size_y // 2).astype(jnp.int32)
    flip_z = (index_z >= size_z // 2).astype(jnp.int32)
    place_y = jnp.where(flip_y == 1, size_y - 1 - index_y, index_y).astype(jnp.int32)
    place_z = jnp.where(flip_z == 1, size_z - 1 - index_z, index_z).astype(jnp.int32)
    sign_y = 1.0 - 2.0 * flip_y.astype(jnp.float32)
    sign_z = 1.0 - 2.0 * flip_z.astype(jnp.float32)
    flags = jnp.stack((flip_y, flip_z))
    merged = size_z == 2
    spans = size_y // 2
    half = vectors // 2

    shares = size_v if rows % (8 * size_v) == 0 else 1
    share_rows = rows // shares
    share = lax.axis_index("vec").astype(jnp.int32) if shares > 1 else jnp.int32(0)
    scalars = jnp.stack((wavenumber[0], sign_y, sign_z))
    own_y, own_z, sent = prepare(
        flags, scalars, share[None], share_rows, mean_flow, viscosity, viscosity_slope
    )
    turn = [[(i, (i + k) % shares) for i in range(shares)] for k in range(shares)]
    pieces = []
    for b in range(spans):
        for mirrored in (False, True):
            if not b and not mirrored:
                continue
            got = lax.ppermute(sent, "gy", partner_pairs(size_y, b, mirrored))
            pieces += [got] + [lax.ppermute(got, "vec", turn[k]) for k in range(1, shares)]
    places = jnp.stack(
        [(place_y ^ b) * rows for b in range(spans)]
        + [((share - k) % shares) * share_rows for k in range(shares)]
    )
    if merged:
        near_z, far_z = own_z, lax.ppermute(own_z, "gz", partner_pairs(size_z, 0, True))
    else:
        near_z, far_z = gather_coefficients(own_z, "gz", flip_z == 1, 2)
    planes = forcing.reshape(vectors * components, rows, cols)
    count = half * components

    def oriented(other, token):
        def picks(flags):
            which = 1 - flags[1] if other else flags[1]
            return [(which * count, count, 0)]

        return orient_planes(planes, flags, picks, 1, count, 0.25, token, "orient_field")

    sent_field = oriented(True, sent)
    flows = orient_planes(
        mean_flow, flags, lambda flags: [(0, 1, 0), (3, 6, 1)], 2, 7, 1.0, sent_field, "orient_flow"
    )
    kept_field = oriented(False, flows)
    coefs = (near_z, far_z, flows, own_y, pieces)

    high, low = folded_tables(2 * half_rows)
    slabs = [
        np.concatenate([t[:, s : s + rows] for t in (high, low)], axis=1)
        for s in range(0, half_rows, rows)
    ]
    pair_y = lax.dynamic_index_in_dim(jnp.asarray(np.stack(slabs)), place_y, 0, keepdims=False)
    table_y = jnp.concatenate((pair_y[:, :rows], pair_y[:, :rows], pair_y[:, rows:], pair_y[:, rows:]), axis=1)
    high, low = folded_tables(2 * half_cols)
    slabs = np.stack([np.stack([t[:, s : s + cols].T for t in (high, low)]) for s in range(0, half_cols, cols)])
    if size_z == 2:
        high_z, low_z = jnp.asarray(slabs[0, 0]), jnp.asarray(slabs[0, 1])
    else:
        pair_z = lax.dynamic_index_in_dim(jnp.asarray(slabs), place_z, 0, keepdims=False)
        high_z, low_z = pair_z[0], pair_z[1]
    tables = (table_y, high_z, low_z)

    def apply(variable, field, token, split=False):
        return apply_variable(variable, merged, split, shares, half_cols, scalars, places, field, tables, coefs, token)

    mirror_y, mirror_z = partner_pairs(size_y, 0, True), partner_pairs(size_z, 0, True)
    if merged and size_y == 4 and half == 1:
        return pipeline(apply, sent_field, kept_field, places, flags, mirror_y, mirror_z)

    def contribution(variable, field):
        parts = []
        for n in range(half):
            got = apply(variable, field[n * components : (n + 1) * components], scalars)
            if merged:
                parts.append(got[0])
            else:
                full = jnp.zeros((2, half_rows, half_cols), jnp.float32)
                full = lax.dynamic_update_slice_in_dim(full, got[0], place_z * cols, 2)
                start = place_y * rows
                strip = lax.dynamic_slice_in_dim(full, start, rows, 1) + got[1]
                parts.append(lax.dynamic_update_slice_in_dim(full, strip, start, 1))
        return halve(jnp.concatenate(parts), "gz", place_z, 2)

    kept_out, sent_out = [], []
    for variable in range(4):
        arrived = lax.ppermute(contribution(variable, sent_field), "gz", mirror_z)
        kept = contribution(variable, kept_field) + Z_SIGNS[variable] * arrived
        kept = halve(kept, "gy", place_y, 1)
        kept = kept + Y_SIGNS[variable] * lax.ppermute(kept, "gy", mirror_y)
        back = Z_SIGNS[variable] * lax.ppermute(kept, "gz", mirror_z)
        kept_out.append(kept.reshape(half, 2, rows, cols))
        sent_out.append(back.reshape(half, 2, rows, cols))
    kept = jnp.concatenate(kept_out, axis=1)
    back = jnp.concatenate(sent_out, axis=1)
    first = jnp.where(flip_z == 1, back, kept)
    second = jnp.where(flip_z == 1, kept, back)
    both = jnp.concatenate((first, second)).reshape(vectors * components, rows, cols)
    every = lambda flags: [(0, vectors * components, 0)]
    out = orient_planes(both, flags, every, 1, vectors * components, 1.0, scalars, "orient_response")
    return out.reshape(forcing.shape)


def pipeline(apply, sent_field, kept_field, places, flags, mirror_y, mirror_z):
    rows, cols = sent_field.shape[1:]
    neighbour_y = partner_pairs(4, 1, False)
    token = kept_field
    kept, moving = {}, {}
    response = None

    def chunks(n):
        return ((n, 0), (n, 1)) if n in SPLIT else ((n, 0),)

    for step, *key in ORDER:
        key = tuple(key)
        n = key[0]
        if step in "SK":
            parts = apply(n, sent_field if step == "S" else kept_field, token, n in SPLIT)
            token = parts[0]
            for chunk, part in zip(chunks(n), parts):
                if step == "S":
                    moving[chunk] = lax.ppermute(part, "gz", mirror_z)
                else:
                    kept[chunk] = part
            continue
        if step == "W":
            sources = [kept[c] for c in chunks(n)], [moving[c] for c in chunks(n)]
            response = token = finish(n, flags, *sources, response, token)
            continue
        small = (kept[key].shape[0], rows, cols)
        pair = (kept[key], moving[key])
        if step == "X":
            kept[key], token = small_call(
                functools.partial(fold_kernel, Z_SIGNS[n]), (small, small), pair, token, "fold_x", (places,)
            )
            moving[key] = lax.ppermute(token, "gy", neighbour_y)
        else:
            sign, axis, partners = (1.0, "gy", mirror_y) if step == "Y" else (Y_SIGNS[n], "gz", mirror_z)
            kernel = functools.partial(add_kernel, sign)
            (token,) = small_call(kernel, (small,), pair, token, "fold_y" if step == "Y" else "fold_m")
            kept[key] = token
            moving[key] = lax.ppermute(token, axis, partners)
    return response


SPLIT = (3, 2)
ORDER = (
    ("S", 3), ("S", 0), ("K", 3), ("X", 3, 0), ("X", 3, 1), ("S", 1),
    ("K", 0), ("Y", 3, 0), ("Y", 3, 1), ("X", 0, 0), ("S", 2), ("K", 1),
    ("M", 3, 0), ("Y", 0, 0), ("M", 3, 1), ("X", 1, 0), ("K", 2), ("X", 2, 0),
    ("Y", 1, 0), ("M", 0, 0), ("X", 2, 1), ("Y", 2, 0), ("Y", 2, 1), ("M", 1, 0),
    ("W", 3), ("M", 2, 0), ("W", 0), ("M", 2, 1), ("W", 1), ("W", 2),
)


def solution(mesh):
    placed = (
        P(("wave", "vec"), None, "gy", "gz"),
        P("wave"),
        P(None, "gy", "gz"),
        P("gy", "gz"),
        P(None, "gy", "gz"),
    )
    return jax.shard_map(
        shards,
        mesh=mesh,
        in_specs=placed,
        out_specs=P(("wave", "vec"), None, "gy", "gz"),
        check_vma=False,
    )
```

```python
import functools
import math

import jax
import jax.numpy as jnp
import numpy as np
from jax import lax
from jax.experimental import pallas as pl
from jax.experimental.pallas import tpu as pltpu
from jax.sharding import PartitionSpec as P


Y_SIGNS = (1.0, -1.0, 1.0, 1.0)
Z_SIGNS = (1.0, 1.0, -1.0, 1.0)
ROW_STEP = 16
WHOLE, PARTS, SLABS = range(3)


def angle_table(points):
    last = points - 1
    row = np.arange(points)[:, None]
    col = np.arange(points)[None, :]
    unit = math.pi / (2.0 * last)
    sine_row = np.sin(2.0 * unit * np.minimum(row, last - row))
    total = row + col
    half_sum = np.sin(unit * np.minimum(total, 2 * last - total))
    half_diff = np.sin(unit * (row - col))
    parity = 1.0 - 2.0 * (total % 2)
    weight = np.where((col == 0) | (col == last), 0.5, 1.0)
    same = row == col
    denominator = np.where(same, 1.0, 2.0 * half_sum * half_diff)
    offdiag = np.where(same, 0.0, math.pi / last * sine_row * parity * weight / denominator)
    return offdiag - np.diag(offdiag.sum(axis=1))


def table_lines(points):
    last, half = points - 1, points // 2
    offset = np.arange(-last, 2 * last + 1)
    angle = offset * (math.pi / (2.0 * last))
    singular = offset % (2 * last) == 0
    cot = np.where(singular, 0.0, np.cos(angle) / np.where(singular, 1.0, np.sin(angle)))
    index = np.arange(points)
    weight = np.where((index == 0) | (index == last), 0.5, 1.0)
    row = index[:, None]
    lines = ((cot[row - index[None, :] + last] - cot[row + index[None, :] + last]) * weight).sum(axis=1)
    table = angle_table(points)
    diagonal = (table * table.T).sum(axis=1)
    return np.stack((lines[:half], lines[::-1][:half], diagonal[:half])).astype(np.float32)


def table_block(points, i, j, here, mirrored, other, diagonal):
    last = points - 1
    unit = math.pi / (2.0 * last)

    def sine_cosine(count):
        small = jnp.minimum(count, last - count)
        x = unit * small.astype(jnp.float32)
        z = x * x
        sine = x * (1.0 + z * (-1.0 / 6.0 + z * (1.0 / 120.0 + z * (-1.0 / 5040.0 + z * (1.0 / 362880.0)))))
        cosine = 1.0 + z * (
            -0.5 + z * (1.0 / 24.0 + z * (-1.0 / 720.0 + z * (1.0 / 40320.0 - z * (1.0 / 3628800.0))))
        )
        swap = count > last - count
        return jnp.where(swap, cosine, sine), jnp.where(swap, sine, cosine)

    apart, total = i - j, i + j
    sine_a, cosine_a = sine_cosine(jnp.abs(apart))
    sine_a = jnp.where(apart < 0, -sine_a, sine_a)
    sine_t, cosine_t = sine_cosine(total)
    same, origin = apart == 0, total == 0
    inverse_a = 1.0 / jnp.where(same, 1.0, sine_a)
    inverse_t = 1.0 / jnp.where(origin, 1.0, sine_t)
    secant_a, secant_t = 1.0 / cosine_a, 1.0 / cosine_t
    sum_near = jnp.where(same, 0.0, cosine_a * inverse_a) + jnp.where(origin, 0.0, cosine_t * inverse_t)
    sum_far = sine_a * secant_a + sine_t * secant_t
    factor = jnp.where(total % 2 == 0, unit, -unit) * jnp.where(j == 0, 0.5, 1.0)
    square = factor * unit
    second_near = square * (sum_near * (here - other) - 2.0 * inverse_a * inverse_a)
    second_near = jnp.where(same, diagonal, second_near)
    second_far = -square * (sum_far * (mirrored - other) - 2.0 * secant_t * secant_t)
    second_near = jnp.where(i == 0, 0.0, second_near)
    second_far = jnp.where(i == 0, 0.0, second_far)
    return factor * sum_near, -factor * sum_far, second_near, second_far


def table_kernel(points_y, points_z, starts, rows_y, cols_y, rows_z, cols_z, token, table_y, high_z, low_z):
    half_y, half_z = points_y // 2, points_z // 2
    width = table_y.shape[1] // 4
    depth = high_z.shape[0]
    step = 16

    @pl.loop(0, half_y // step)
    def _(index):
        start = pl.multiple_of(index * step, step)
        span = pl.ds(start, step)
        shape = (step, width)
        i = start + lax.broadcasted_iota(jnp.int32, shape, 0)
        j = starts[0] + lax.broadcasted_iota(jnp.int32, shape, 1)
        lines = [jnp.broadcast_to(cols_y[n, span, :], shape) for n in range(3)]
        other = jnp.broadcast_to(rows_y[0:1, :], shape)
        for kind, block in enumerate(table_block(points_y, i, j, *lines[:2], other, lines[2])):
            high, low = split_high_low(block)
            place = pl.ds(pl.multiple_of(kind * half_y + start, step), step)
            for n, part in enumerate((high, high, low, low)):
                table_y[place, n * width : (n + 1) * width] = part

    @pl.loop(0, depth // step)
    def _(index):
        start = pl.multiple_of(index * step, step)
        span = pl.ds(start, step)
        shape = (step, half_z)
        j = starts[1] + start + lax.broadcasted_iota(jnp.int32, shape, 0)
        i = lax.broadcasted_iota(jnp.int32, shape, 1)
        lines = [jnp.broadcast_to(rows_z[n : n + 1, :], shape) for n in range(3)]
        other = jnp.broadcast_to(cols_z[0, span, :], shape)
        for kind, block in enumerate(table_block(points_z, i, j, *lines[:2], other, lines[2])):
            high, low = split_high_low(block)
            high_z[span, kind * half_z : (kind + 1) * half_z] = high
            low_z[span, kind * half_z : (kind + 1) * half_z] = low


def make_tables(rows, cols, half_rows, half_cols, place_y, place_z, token):
    lines_y, lines_z = table_lines(2 * half_rows), table_lines(2 * half_cols)
    smem, vmem = pl.BlockSpec(memory_space=pltpu.SMEM), pl.BlockSpec(memory_space=pltpu.VMEM)
    own_y = lax.dynamic_slice_in_dim(jnp.asarray(lines_y[0:1]), place_y * rows, rows, 1)
    own_z = lax.dynamic_slice_in_dim(jnp.asarray(lines_z[0:1, :, None]), place_z * cols, cols, 1)
    shapes = ((4 * half_rows, 4 * rows), (cols, 4 * half_cols), (cols, 4 * half_cols))
    call = pl.pallas_call(
        functools.partial(table_kernel, 2 * half_rows, 2 * half_cols),
        out_shape=tuple(vmem_result(s, jnp.bfloat16) for s in shapes),
        in_specs=[smem] + [vmem] * 4 + [pl.BlockSpec(memory_space=pl.ANY)],
        out_specs=(vmem,) * 3,
        compiler_params=pltpu.CompilerParams(vmem_limit_bytes=10 << 20),
        cost_estimate=pl.CostEstimate(flops=1 << 27, bytes_accessed=1 << 20, transcendentals=0),
        name="tables",
    )
    starts = jnp.stack((place_y * rows, place_z * cols))
    return call(starts, own_y, jnp.asarray(lines_y[:, :, None]), jnp.asarray(lines_z), own_z, token)


def split_high_low(values):
    high = values.astype(jnp.bfloat16)
    low = (values - high.astype(jnp.float32)).astype(jnp.bfloat16)
    return high, low


def dot(left, right):
    return jnp.dot(left, right, preferred_element_type=jnp.float32)


def in_vmem(values):
    return pltpu.with_memory_space_constraint(values, pltpu.VMEM)


def in_hbm(values):
    return pltpu.with_memory_space_constraint(values, pltpu.HBM)


def vmem_result(shape, dtype=jnp.float32):
    return pltpu.VMEM(shape, dtype)


def hbm_result(shape):
    return pltpu.HBM(shape, jnp.float32)


def exchange(size):
    row = lax.broadcasted_iota(jnp.int32, (size, size), 0)
    col = lax.broadcasted_iota(jnp.int32, (size, size), 1)
    return jnp.where(row + col == size - 1, 1.0, 0.0).astype(jnp.bfloat16)


def three_parts(values):
    high = values.astype(jnp.bfloat16)
    rest = values - high.astype(jnp.float32)
    middle = rest.astype(jnp.bfloat16)
    low = (rest - middle.astype(jnp.float32)).astype(jnp.bfloat16)
    return high, middle, low


def store_oriented(flags, planes, out, scale):
    count, rows, cols = planes.shape
    planes = scale * planes

    @pl.when(flags[1] == 0)
    def _():
        out[...] = planes

    @pl.when(flags[1] == 1)
    def _():
        flat = planes.reshape(count * rows, cols)
        matrix = exchange(cols)
        high, middle, low = (dot(part, matrix) for part in three_parts(flat))
        out[...] = ((high + middle) + low).reshape(count, rows, cols)

    @pl.when(flags[0] == 1)
    def _():
        matrix = exchange(rows)
        for n in range(count):
            high, middle, low = (dot(matrix, part) for part in three_parts(out[n]))
            out[n] = (high + middle) + low


def orient_kernel(scale, picks, flags, values, token, out, planes, sems):
    copies = []
    for n, (source, count, place) in enumerate(picks(flags)):
        copies.append(
            pltpu.make_async_copy(values.at[pl.ds(source, count)], planes.at[pl.ds(place, count)], sems.at[n])
        )
    for copy in copies:
        copy.start()
    for copy in copies:
        copy.wait()
    store_oriented(flags, planes[...], out, scale)


def orient_planes(values, flags, picks, runs, count, scale, token):
    shape = (count,) + values.shape[1:]
    anywhere, hbm = pl.BlockSpec(memory_space=pl.ANY), pl.BlockSpec(memory_space=pltpu.HBM)
    return pl.pallas_call(
        functools.partial(orient_kernel, scale, picks),
        out_shape=vmem_result(shape),
        in_specs=[pl.BlockSpec(memory_space=pltpu.SMEM), hbm, anywhere],
        out_specs=pl.BlockSpec(memory_space=pltpu.VMEM),
        scratch_shapes=[pltpu.VMEM(shape, jnp.float32), pltpu.SemaphoreType.DMA((runs,))],
        compiler_params=pltpu.CompilerParams(vmem_limit_bytes=16 << 20),
        cost_estimate=pl.CostEstimate(flops=count << 24, bytes_accessed=count << 19, transcendentals=0),
    )(flags, in_hbm(values), token)


def prepare_kernel(flags, signs, share, flow, viscosity, slope, own_y, own_z, sent, work, oriented, sems):
    copies = (
        pltpu.make_async_copy(viscosity, work.at[0], sems.at[0]),
        pltpu.make_async_copy(slope, work.at[pl.ds(1, 2)], sems.at[1]),
        pltpu.make_async_copy(flow.at[pl.ds(1, 2)], work.at[pl.ds(3, 2)], sems.at[2]),
    )
    for copy in copies:
        copy.start()
    for copy in copies:
        copy.wait()
    for n in (1, 2):
        work[n] = signs[n] * (work[n] - work[n + 2])
    store_oriented(flags, work[0:3], oriented, 1.0)
    own_y[...] = oriented[0:2]
    own_z[0] = oriented[0]
    own_z[1] = oriented[2]
    rows = sent.shape[1]
    span = pl.ds(pl.multiple_of(share[0] * rows, rows), rows)
    for n in (0, 1):
        sent[n] = oriented[n, span, :]


def prepare(flags, signs, share, share_rows, flow, viscosity, slope):
    rows, cols = viscosity.shape
    smem, hbm = pl.BlockSpec(memory_space=pltpu.SMEM), pl.BlockSpec(memory_space=pltpu.HBM)
    shapes = ((2, rows, cols), (2, rows, cols), (2, share_rows, cols))
    return pl.pallas_call(
        prepare_kernel,
        out_shape=tuple(vmem_result(s) for s in shapes),
        in_specs=[smem] * 3 + [hbm] * 3,
        out_specs=(pl.BlockSpec(memory_space=pltpu.VMEM),) * 3,
        scratch_shapes=[
            pltpu.VMEM((5, rows, cols), jnp.float32),
            pltpu.VMEM((3, rows, cols), jnp.float32),
            pltpu.SemaphoreType.DMA((3,)),
        ],
        compiler_params=pltpu.CompilerParams(vmem_limit_bytes=10 << 20),
        cost_estimate=pl.CostEstimate(flops=1 << 26, bytes_accessed=3 << 20, transcendentals=0),
        name="prepare",
    )(flags, signs, share, in_hbm(flow), in_hbm(viscosity), in_hbm(slope))


def operator_kernel(variable, merged, layout, shares, spans, scalars, places, *refs):
    refs = list(refs)
    field, table_y, high_z, low_z = refs[:4]
    near_z, far_z, flows, own_y = refs[4:8]
    taken = 8
    plane = min(variable, 2)
    near_y, far_y = [None], []
    for b in range(spans):
        if b:
            near_y.append(refs[taken : taken + shares])
            taken += shares
        far_y.append(refs[taken : taken + shares])
        taken += shares
    taken += 1
    outs = refs[taken:-2]
    out_z = None if merged else outs[1]
    scratch_y, scratch_z = refs[-2:]

    rows, cols = field.shape[1:]
    half_rows = spans * rows
    half_cols = scratch_z.shape[2]
    share_rows = rows // shares
    stream, sign_y, sign_z = scalars[0], scalars[1], scalars[2]
    fold_y, fold_z = Y_SIGNS[variable], Z_SIGNS[variable]
    u, v, w, p = 0, 2, 4, 6
    base = 2 * variable
    step_y = min(ROW_STEP, share_rows)
    step_z = min(ROW_STEP, rows)

    def target(part, b):
        if layout == SLABS:
            return outs[b].at[part], 0
        first = pl.multiple_of(places[b], rows)
        return (outs[part].at[0] if layout == PARTS else outs[0].at[part]), first


    def along_y(part, source, kinds):
        high, low = split_high_low(field[source + part])
        stacked = jnp.concatenate((high, low, high, low), axis=0)

        @pl.loop(0, kinds // 2)
        def _(index):
            span = pl.ds(pl.multiple_of(index * 2 * half_rows, 2 * half_rows), 2 * half_rows)
            scratch_y[span, :] = dot(table_y[span, :], stacked)

    def along_z(source, kinds):
        both = field[source : source + 2].reshape(2 * rows, cols)
        high, low = split_high_low(both)

        @pl.loop(0, kinds)
        def _(kind):
            span = pl.ds(pl.multiple_of(kind * half_cols, half_cols), half_cols)
            total = dot(high, high_z[:, span])
            total = total + dot(low, high_z[:, span])
            total = total + dot(high, low_z[:, span])
            scratch_z[kind] = total

    def at(kind, start):
        return scratch_y[pl.ds(kind * half_rows + start, step_y), :]

    def rows_y(part, body):
        for b in range(spans):
            out, slab_first = target(part, b)

            @pl.loop(0, rows // step_y)
            def _(index, b=b, out=out, slab_first=slab_first):
                inner = pl.multiple_of(index * step_y, step_y)
                start = pl.multiple_of(places[b] + inner, step_y)
                body(out, pl.ds(pl.multiple_of(slab_first + inner, step_y), step_y), start)

    for part in (0, 1):
        if variable < 3:
            along_y(part, base, 4)
            for b in range(spans):
                for t in range(shares):
                    offset = pl.multiple_of(places[spans + t], share_rows)
                    out, slab_first = target(part, b)

                    @pl.loop(0, share_rows // step_y)
                    def _(index, b=b, t=t, offset=offset, out=out, slab_first=slab_first):
                        inner = pl.multiple_of(index * step_y, step_y)
                        start = pl.multiple_of(places[b] + offset + inner, step_y)
                        place = pl.multiple_of(slab_first + offset + inner, step_y)
                        local = pl.ds(inner, step_y)
                        if b:
                            viscous, slope = near_y[b][t][0, local, :], near_y[b][t][1, local, :]
                        else:
                            span = pl.ds(pl.multiple_of(offset + inner, step_y), step_y)
                            viscous, slope = own_y[0, span, :], own_y[1, span, :]
                        near = viscous * at(2, start) + slope * at(0, start)
                        far = far_y[b][t][0, local, :] * at(3, start) - far_y[b][t][1, local, :] * at(1, start)
                        out[pl.ds(place, step_y), :] = near + fold_y * far

            if variable == 1:
                along_y(part, p, 2)

                def push(out, span, start):
                    out[span, :] = out[span, :] - sign_y * (at(0, start) - at(1, start))

                rows_y(part, push)
        else:
            along_y(part, v, 2)

            def diverge(out, span, start):
                out[span, :] = sign_y * (at(0, start) + at(1, start))

            rows_y(part, diverge)

    def add_own(part, start, values):
        out, slab_first = target(part, 0)
        span = pl.ds(pl.multiple_of(slab_first + start, step_z), step_z)
        out[span, :] = out[span, :] + values

    def add_z(part, start, values):
        if merged:
            add_own(part, start, values)
        else:
            span = pl.ds(start, step_z)
            out_z[part, span, :] = out_z[part, span, :] + values

    if not merged:
        out_z[...] = jnp.zeros_like(out_z)

    def rows_z(body):
        @pl.loop(0, rows // step_z)
        def _(index):
            start = pl.multiple_of(index * step_z, step_z)
            for part in (0, 1):
                body(part, start)

    def at_z(kind, part, start):
        return scratch_z[kind, pl.ds(part * rows + start, step_z), :]

    def point(plane, start):
        return field[plane, pl.ds(start, step_z), :]

    turn = (1.0, -1.0)
    if variable < 3:
        along_z(base, 4)

        def both(part, start):
            span = pl.ds(start, step_z)
            near = near_z[0, span, :] * at_z(2, part, start) + near_z[1, span, :] * at_z(0, part, start)
            far = far_z[0, span, :] * at_z(3, part, start) - far_z[1, span, :] * at_z(1, part, start)
            add_z(part, start, near + fold_z * far)
            moved = turn[part] * stream * flows[0, span, :] * point(base + 1 - part, start)
            made = flows[1 + 2 * plane, span, :] * point(v + part, start) + flows[2 + 2 * plane, span, :] * point(w + part, start)
            lost = own_y[0, span, :] * (stream * stream) * point(base + part, start)
            values = moved - made - lost
            if variable == 0:
                values = values + turn[part] * stream * point(p + 1 - part, start)
            add_own(part, start, values)

        rows_z(both)
        if variable == 2:
            along_z(p, 2)

            def push_z(part, start):
                add_z(part, start, -sign_z * (at_z(0, part, start) - at_z(1, part, start)))

            rows_z(push_z)
    else:
        along_z(w, 2)

        def diverge_z(part, start):
            add_z(part, start, sign_z * (at_z(0, part, start) + at_z(1, part, start)))
            add_own(part, start, -turn[part] * stream * point(u + 1 - part, start))

        rows_z(diverge_z)


def call_in_vmem(kernel, out_shapes, scalars, arrays, token, flops, scratch=(), limit=8):
    vmem = pl.BlockSpec(memory_space=pltpu.VMEM)
    smem = pl.BlockSpec(memory_space=pltpu.SMEM)
    call = pl.pallas_call(
        kernel,
        out_shape=tuple(vmem_result(s) for s in out_shapes),
        in_specs=[smem] * len(scalars) + [vmem] * len(arrays) + [pl.BlockSpec(memory_space=pl.ANY)],
        out_specs=tuple(vmem for _ in out_shapes),
        scratch_shapes=list(scratch),
        compiler_params=pltpu.CompilerParams(vmem_limit_bytes=limit << 20),
        cost_estimate=pl.CostEstimate(flops=flops, bytes_accessed=3 << 20, transcendentals=0),
    )
    arrays = [in_vmem(a) for a in arrays]
    return call(*scalars, *arrays, token)


def apply_variable(variable, merged, layout, shares, half_cols, scalars, places, field, tables, coefs, token):
    near_z, far_z, flows, own_y, pieces = coefs
    rows, cols = field.shape[1:]
    half_rows = tables[0].shape[0] // 4
    spans = half_rows // rows
    shapes = {
        WHOLE: [(2, half_rows, cols)],
        PARTS: [(1, half_rows, cols)] * 2,
        SLABS: [(2, rows, cols)] * spans,
    }[layout]
    if not merged:
        shapes.append((2, rows, half_cols))
    work = 8 * 2 * (4 * half_rows * 4 * rows * cols + 3 * rows * cols * 4 * half_cols) // 4
    return call_in_vmem(
        functools.partial(operator_kernel, variable, merged, layout, shares, spans),
        shapes,
        (scalars, places),
        (field, *tables, near_z, far_z, flows, own_y, *pieces),
        token,
        work,
        (
            pltpu.VMEM((4 * half_rows, cols), jnp.float32),
            pltpu.VMEM((4, 2 * rows, half_cols), jnp.float32),
        ),
        20,
    )


def fold_kernel(sign, places, mine, theirs, token, kept, sent):
    rows = kept.shape[1]
    for part in range(mine.shape[0]):
        for slab, out in ((0, kept), (1, sent)):
            span = pl.ds(pl.multiple_of(places[slab], rows), rows)
            out[part] = mine[part, span, :] + sign * theirs[part, span, :]


def add_kernel(sign, mine, theirs, token, out):
    out[...] = mine[...] + sign * theirs[...]


def small_call(kernel, out_shapes, arrays, token, scalars=()):
    return call_in_vmem(kernel, out_shapes, scalars, arrays, token, 1 << 20)


def finish_kernel(sign, count, first, flags, *refs):
    kept, back, out, staged, sems = refs[:count], refs[count : 2 * count], refs[-3], refs[-2], refs[-1]
    for vector, (sources, factor) in enumerate(((kept, 1.0), (back, sign))):
        place = flags[1] if vector == 0 else 1 - flags[1]
        values = jnp.concatenate([ref[...] for ref in sources]) if count > 1 else sources[0][...]
        store_oriented(flags, values, staged.at[vector], factor)
        pltpu.make_async_copy(
            staged.at[vector], out.at[place, pl.ds(first, 2)], sems.at[vector]
        ).start()
    for vector in (0, 1):
        place = flags[1] if vector == 0 else 1 - flags[1]
        pltpu.make_async_copy(
            staged.at[vector], out.at[place, pl.ds(first, 2)], sems.at[vector]
        ).wait()


def finish(variable, flags, kept, back, response, token):
    rows, cols = kept[0].shape[1:]
    anywhere, vmem = pl.BlockSpec(memory_space=pl.ANY), pl.BlockSpec(memory_space=pltpu.VMEM)
    hbm = pl.BlockSpec(memory_space=pltpu.HBM)
    count = len(kept)
    arrays = [in_vmem(a) for a in (*kept, *back)]
    specs = [pl.BlockSpec(memory_space=pltpu.SMEM)] + [vmem] * len(arrays)
    extras = [token] if token is not response else []
    extras += [] if response is None else [in_hbm(response)]
    arrays += extras
    specs += [anywhere] * (len(extras) - 1) + [anywhere if response is None else hbm]
    return pl.pallas_call(
        functools.partial(finish_kernel, Z_SIGNS[variable], count, 2 * variable),
        out_shape=hbm_result((2, 8, rows, cols)),
        in_specs=specs,
        out_specs=hbm,
        scratch_shapes=[pltpu.VMEM((2, 2, rows, cols), jnp.float32), pltpu.SemaphoreType.DMA((2,))],
        input_output_aliases={} if response is None else {len(arrays): 0},
        compiler_params=pltpu.CompilerParams(vmem_limit_bytes=10 << 20),
        cost_estimate=pl.CostEstimate(flops=1 << 26, bytes_accessed=2 << 20, transcendentals=0),
    )(flags, *arrays)


def partner_pairs(size, bit, mirrored):
    pairs = []
    for i in range(size):
        far_end = i >= size // 2
        place = (size - 1 - i if far_end else i) ^ bit
        pairs.append((i, size - 1 - place if far_end != mirrored else place))
    return pairs


def halve(values, axis_name, position, dim):
    size = lax.axis_size(axis_name)
    bit = size // 4
    while bit:
        length = values.shape[dim] // 2
        upper = (position // bit) % 2
        kept = lax.dynamic_slice_in_dim(values, upper * length, length, dim)
        sent = lax.dynamic_slice_in_dim(values, (1 - upper) * length, length, dim)
        values = kept + lax.ppermute(sent, axis_name, partner_pairs(size, bit, False))
        bit //= 2
    return values


def gather_coefficients(planes, axis_name, flipped, dim):
    size = lax.axis_size(axis_name)
    gathered = lax.all_gather(planes, axis_name)
    low = jnp.concatenate([gathered[i] for i in range(size // 2)], axis=dim)
    high = jnp.concatenate([gathered[size - 1 - i] for i in range(size // 2)], axis=dim)
    return jnp.where(flipped, high, low), jnp.where(flipped, low, high)


def shards(forcing, wavenumber, mean_flow, viscosity, viscosity_slope):
    vectors, components, rows, cols = forcing.shape
    size_y, size_z, size_v = lax.axis_size("gy"), lax.axis_size("gz"), lax.axis_size("vec")
    half_rows, half_cols = rows * size_y // 2, cols * size_z // 2
    index_y, index_z = lax.axis_index("gy"), lax.axis_index("gz")
    flip_y = (index_y >= size_y // 2).astype(jnp.int32)
    flip_z = (index_z >= size_z // 2).astype(jnp.int32)
    place_y = jnp.where(flip_y == 1, size_y - 1 - index_y, index_y).astype(jnp.int32)
    place_z = jnp.where(flip_z == 1, size_z - 1 - index_z, index_z).astype(jnp.int32)
    sign_y = 1.0 - 2.0 * flip_y.astype(jnp.float32)
    sign_z = 1.0 - 2.0 * flip_z.astype(jnp.float32)
    flags = jnp.stack((flip_y, flip_z))
    merged = size_z == 2
    spans = size_y // 2
    half = vectors // 2

    shares = size_v if rows % (8 * size_v) == 0 else 1
    share_rows = rows // shares
    share = lax.axis_index("vec").astype(jnp.int32) if shares > 1 else jnp.int32(0)
    scalars = jnp.stack((wavenumber[0], sign_y, sign_z))
    own_y, own_z, sent = prepare(
        flags, scalars, share[None], share_rows, mean_flow, viscosity, viscosity_slope
    )
    turn = [[(i, (i + k) % shares) for i in range(shares)] for k in range(shares)]
    pieces = []
    for b in range(spans):
        for mirrored in (False, True):
            if not b and not mirrored:
                continue
            got = lax.ppermute(sent, "gy", partner_pairs(size_y, b, mirrored))
            pieces += [got] + [lax.ppermute(got, "vec", turn[k]) for k in range(1, shares)]
    places = jnp.stack(
        [(place_y ^ b) * rows for b in range(spans)]
        + [((share - k) % shares) * share_rows for k in range(shares)]
    )
    if merged:
        near_z, far_z = own_z, lax.ppermute(own_z, "gz", partner_pairs(size_z, 0, True))
    else:
        near_z, far_z = gather_coefficients(own_z, "gz", flip_z == 1, 2)
    tables = make_tables(rows, cols, half_rows, half_cols, place_y, place_z, sent)
    planes = forcing.reshape(vectors * components, rows, cols)
    count = half * components

    def oriented(other, token):
        def picks(flags):
            which = 1 - flags[1] if other else flags[1]
            return [(which * count, count, 0)]

        return orient_planes(planes, flags, picks, 1, count, 0.25, token)

    sent_field = oriented(True, tables[0])
    flows = orient_planes(mean_flow, flags, lambda flags: [(0, 1, 0), (3, 6, 1)], 2, 7, 1.0, sent_field)
    kept_field = oriented(False, flows)
    coefs = (near_z, far_z, flows, own_y, pieces)

    def apply(variable, field, token, layout=WHOLE):
        return apply_variable(variable, merged, layout, shares, half_cols, scalars, places, field, tables, coefs, token)

    mirror_y, mirror_z = partner_pairs(size_y, 0, True), partner_pairs(size_z, 0, True)
    if merged and size_y == 4 and half == 1:
        return pipeline(apply, sent_field, kept_field, places, flags, mirror_y, mirror_z)

    def contribution(variable, field):
        parts = []
        for n in range(half):
            got = apply(variable, field[n * components : (n + 1) * components], scalars)
            if merged:
                parts.append(got[0])
            else:
                full = jnp.zeros((2, half_rows, half_cols), jnp.float32)
                full = lax.dynamic_update_slice_in_dim(full, got[0], place_z * cols, 2)
                start = place_y * rows
                strip = lax.dynamic_slice_in_dim(full, start, rows, 1) + got[1]
                parts.append(lax.dynamic_update_slice_in_dim(full, strip, start, 1))
        return halve(jnp.concatenate(parts), "gz", place_z, 2)

    kept_out, sent_out = [], []
    for variable in range(4):
        arrived = lax.ppermute(contribution(variable, sent_field), "gz", mirror_z)
        kept = contribution(variable, kept_field) + Z_SIGNS[variable] * arrived
        kept = halve(kept, "gy", place_y, 1)
        kept = kept + Y_SIGNS[variable] * lax.ppermute(kept, "gy", mirror_y)
        back = Z_SIGNS[variable] * lax.ppermute(kept, "gz", mirror_z)
        kept_out.append(kept.reshape(half, 2, rows, cols))
        sent_out.append(back.reshape(half, 2, rows, cols))
    kept = jnp.concatenate(kept_out, axis=1)
    back = jnp.concatenate(sent_out, axis=1)
    first = jnp.where(flip_z == 1, back, kept)
    second = jnp.where(flip_z == 1, kept, back)
    both = jnp.concatenate((first, second)).reshape(vectors * components, rows, cols)
    every = lambda flags: [(0, vectors * components, 0)]
    out = orient_planes(both, flags, every, 1, vectors * components, 1.0, scalars)
    return out.reshape(forcing.shape)


def add_all_kernel(sign, mine, near, theirs, token, out):
    out[...] = (mine[...] + near[...]) + sign * theirs[...]


def pipeline(apply, sent_field, kept_field, places, flags, mirror_y, mirror_z):
    rows, cols = sent_field.shape[1:]
    neighbour_y = partner_pairs(4, 1, False)
    token = kept_field
    kept, moving, extra, sends = {}, {}, {}, []
    response = None

    def chunks(n):
        return ((n, 0), (n, 1)) if LAYOUT[n] == PARTS else ((n, 0),)

    def send(values, axis, partners):
        sends[-1].append(axis)
        return lax.ppermute(values, axis, partners)

    def add(kernel, arrays, shape):
        return small_call(kernel, (shape,), arrays, token)[0]

    def act(step, key):
        nonlocal token, response
        n = key[0]
        if step in "SK":
            parts = apply(n, sent_field if step == "S" else kept_field, token, LAYOUT[n])
            token = parts[0]
            if LAYOUT[n] == SLABS:
                arrived = send(parts[1], "gy", neighbour_y)
                (extra if step == "S" else kept)[key] = (parts[0], arrived)
                return
            for chunk, part in zip(chunks(n), parts):
                if step == "S":
                    moving[chunk] = send(part, "gz", mirror_z)
                else:
                    kept[chunk] = part
            return
        if step == "W":
            sources = [kept[c] for c in chunks(n)], [moving[c] for c in chunks(n)]
            response = token = finish(n, flags, *sources, response, token)
            return
        if step == "A":
            token = add(functools.partial(add_kernel, 1.0), extra[key], extra[key][0].shape)
            moving[key] = send(token, "gz", mirror_z)
            return
        if step == "C":
            arrays = (*kept[key], moving[key])
            token = add(functools.partial(add_all_kernel, Z_SIGNS[n]), arrays, arrays[0].shape)
            kept[key] = token
            moving[key] = send(token, "gy", mirror_y)
            return
        small = (kept[key].shape[0], rows, cols)
        pair = (kept[key], moving[key])
        if step == "X":
            kept[key], token = small_call(
                functools.partial(fold_kernel, Z_SIGNS[n]), (small, small), pair, token, (places,)
            )
            moving[key] = send(token, "gy", neighbour_y)
        else:
            sign, axis, partners = (1.0, "gy", mirror_y) if step == "Y" else (Y_SIGNS[n], "gz", mirror_z)
            token = add(functools.partial(add_kernel, sign), pair, small)
            kept[key] = token
            moving[key] = send(token, axis, partners)

    for step, *key in ORDER:
        sends.append([])
        act(step, tuple(key))
    return response


LAYOUT = (PARTS, PARTS, PARTS, PARTS)
ORDER = (
    ("S", 3, 0), ("S", 0, 0), ("K", 3, 0), ("X", 3, 0), ("S", 2, 0), ("Y", 3, 0),
    ("X", 3, 1), ("K", 0, 0), ("X", 0, 0), ("Y", 3, 1), ("S", 1, 0), ("Y", 0, 0),
    ("X", 0, 1), ("K", 2, 0), ("X", 2, 0), ("Y", 0, 1), ("X", 2, 1), ("K", 1, 0),
    ("Y", 2, 0), ("X", 1, 0), ("M", 3, 0), ("M", 0, 0), ("M", 0, 1), ("Y", 2, 1),
    ("X", 1, 1), ("M", 3, 1), ("Y", 1, 0), ("M", 2, 0), ("W", 0), ("Y", 1, 1),
    ("M", 2, 1), ("W", 3), ("M", 1, 0), ("M", 1, 1), ("W", 2), ("W", 1),
)


def solution(mesh):
    placed = (
        P(("wave", "vec"), None, "gy", "gz"),
        P("wave"),
        P(None, "gy", "gz"),
        P("gy", "gz"),
        P(None, "gy", "gz"),
    )

    return jax.shard_map(
        shards,
        mesh=mesh,
        in_specs=placed,
        out_specs=P(("wave", "vec"), None, "gy", "gz"),
        check_vma=False,
    )
```

```python
import functools
import math

import jax
import jax.numpy as jnp
import numpy as np
from jax import lax
from jax.experimental import pallas as pl
from jax.experimental.pallas import tpu as pltpu
from jax.sharding import PartitionSpec as P


Y_SIGNS = (1.0, -1.0, 1.0, 1.0)
Z_SIGNS = (1.0, 1.0, -1.0, 1.0)
ROW_STEP = 16
WHOLE, PARTS, SLABS = range(3)


def angle_table(points):
    last = points - 1
    row = np.arange(points)[:, None]
    col = np.arange(points)[None, :]
    unit = math.pi / (2.0 * last)
    sine_row = np.sin(2.0 * unit * np.minimum(row, last - row))
    total = row + col
    half_sum = np.sin(unit * np.minimum(total, 2 * last - total))
    half_diff = np.sin(unit * (row - col))
    parity = 1.0 - 2.0 * (total % 2)
    weight = np.where((col == 0) | (col == last), 0.5, 1.0)
    same = row == col
    denominator = np.where(same, 1.0, 2.0 * half_sum * half_diff)
    offdiag = np.where(same, 0.0, math.pi / last * sine_row * parity * weight / denominator)
    return offdiag - np.diag(offdiag.sum(axis=1))


def table_lines(points):
    last, half = points - 1, points // 2
    offset = np.arange(-last, 2 * last + 1)
    angle = offset * (math.pi / (2.0 * last))
    singular = offset % (2 * last) == 0
    cot = np.where(singular, 0.0, np.cos(angle) / np.where(singular, 1.0, np.sin(angle)))
    index = np.arange(points)
    weight = np.where((index == 0) | (index == last), 0.5, 1.0)
    row = index[:, None]
    lines = ((cot[row - index[None, :] + last] - cot[row + index[None, :] + last]) * weight).sum(axis=1)
    table = angle_table(points)
    diagonal = (table * table.T).sum(axis=1)
    return np.stack((lines[:half], lines[::-1][:half], diagonal[:half])).astype(np.float32)


def table_block(points, i, j, here, mirrored, other, diagonal):
    last = points - 1
    unit = math.pi / (2.0 * last)

    def sine_cosine(count):
        small = jnp.minimum(count, last - count)
        x = unit * small.astype(jnp.float32)
        z = x * x
        sine = x * (1.0 + z * (-1.0 / 6.0 + z * (1.0 / 120.0 + z * (-1.0 / 5040.0 + z * (1.0 / 362880.0)))))
        cosine = 1.0 + z * (
            -0.5 + z * (1.0 / 24.0 + z * (-1.0 / 720.0 + z * (1.0 / 40320.0 - z * (1.0 / 3628800.0))))
        )
        swap = count > last - count
        return jnp.where(swap, cosine, sine), jnp.where(swap, sine, cosine)

    apart, total = i - j, i + j
    sine_a, cosine_a = sine_cosine(jnp.abs(apart))
    sine_a = jnp.where(apart < 0, -sine_a, sine_a)
    sine_t, cosine_t = sine_cosine(total)
    same, origin = apart == 0, total == 0
    inverse_a = 1.0 / jnp.where(same, 1.0, sine_a)
    inverse_t = 1.0 / jnp.where(origin, 1.0, sine_t)
    secant_a, secant_t = 1.0 / cosine_a, 1.0 / cosine_t
    sum_near = jnp.where(same, 0.0, cosine_a * inverse_a) + jnp.where(origin, 0.0, cosine_t * inverse_t)
    sum_far = sine_a * secant_a + sine_t * secant_t
    factor = jnp.where(total % 2 == 0, unit, -unit) * jnp.where(j == 0, 0.5, 1.0)
    square = factor * unit
    second_near = square * (sum_near * (here - other) - 2.0 * inverse_a * inverse_a)
    second_near = jnp.where(same, diagonal, second_near)
    second_far = -square * (sum_far * (mirrored - other) - 2.0 * secant_t * secant_t)
    second_near = jnp.where(i == 0, 0.0, second_near)
    second_far = jnp.where(i == 0, 0.0, second_far)
    return factor * sum_near, -factor * sum_far, second_near, second_far


def table_kernel(points_y, points_z, starts, rows_y, cols_y, rows_z, cols_z, token, table_y, high_z, low_z):
    half_y, half_z = points_y // 2, points_z // 2
    width = table_y.shape[1] // 4
    depth = high_z.shape[0]
    step = 16

    @pl.loop(0, half_y // step)
    def _(index):
        start = pl.multiple_of(index * step, step)
        span = pl.ds(start, step)
        shape = (step, width)
        i = start + lax.broadcasted_iota(jnp.int32, shape, 0)
        j = starts[0] + lax.broadcasted_iota(jnp.int32, shape, 1)
        lines = [jnp.broadcast_to(cols_y[n, span, :], shape) for n in range(3)]
        other = jnp.broadcast_to(rows_y[0:1, :], shape)
        for kind, block in enumerate(table_block(points_y, i, j, *lines[:2], other, lines[2])):
            high, low = split_high_low(block)
            place = pl.ds(pl.multiple_of(kind * half_y + start, step), step)
            for n, part in enumerate((high, high, low, low)):
                table_y[place, n * width : (n + 1) * width] = part

    @pl.loop(0, depth // step)
    def _(index):
        start = pl.multiple_of(index * step, step)
        span = pl.ds(start, step)
        shape = (step, half_z)
        j = starts[1] + start + lax.broadcasted_iota(jnp.int32, shape, 0)
        i = lax.broadcasted_iota(jnp.int32, shape, 1)
        lines = [jnp.broadcast_to(rows_z[n : n + 1, :], shape) for n in range(3)]
        other = jnp.broadcast_to(cols_z[0, span, :], shape)
        for kind, block in enumerate(table_block(points_z, i, j, *lines[:2], other, lines[2])):
            high, low = split_high_low(block)
            high_z[span, kind * half_z : (kind + 1) * half_z] = high
            low_z[span, kind * half_z : (kind + 1) * half_z] = low


def make_tables(rows, cols, half_rows, half_cols, starts, token):
    lines_y, lines_z = table_lines(2 * half_rows), table_lines(2 * half_cols)
    smem, vmem = pl.BlockSpec(memory_space=pltpu.SMEM), pl.BlockSpec(memory_space=pltpu.VMEM)
    own_y = lax.dynamic_slice_in_dim(jnp.asarray(lines_y[0:1]), starts[0], rows, 1)
    own_z = lax.dynamic_slice_in_dim(jnp.asarray(lines_z[0:1, :, None]), starts[1], cols, 1)
    shapes = ((4 * half_rows, 4 * rows), (cols, 4 * half_cols), (cols, 4 * half_cols))
    return pl.pallas_call(
        functools.partial(table_kernel, 2 * half_rows, 2 * half_cols),
        out_shape=tuple(vmem_result(s, jnp.bfloat16) for s in shapes),
        in_specs=[smem] + [vmem] * 4 + [pl.BlockSpec(memory_space=pl.ANY)],
        out_specs=(vmem,) * 3,
        compiler_params=pltpu.CompilerParams(vmem_limit_bytes=10 << 20),
        cost_estimate=pl.CostEstimate(flops=1 << 27, bytes_accessed=1 << 20, transcendentals=0),
        name="tables",
    )(starts, own_y, jnp.asarray(lines_y[:, :, None]), jnp.asarray(lines_z), own_z, token)


def split_high_low(values):
    high = values.astype(jnp.bfloat16)
    low = (values - high.astype(jnp.float32)).astype(jnp.bfloat16)
    return high, low


def dot(left, right):
    return jnp.dot(left, right, preferred_element_type=jnp.float32)


def in_vmem(values):
    return pltpu.with_memory_space_constraint(values, pltpu.VMEM)


def in_hbm(values):
    return pltpu.with_memory_space_constraint(values, pltpu.HBM)


def vmem_result(shape, dtype=jnp.float32):
    return pltpu.VMEM(shape, dtype)


def hbm_result(shape):
    return pltpu.HBM(shape, jnp.float32)


def exchange(size):
    row = lax.broadcasted_iota(jnp.int32, (size, size), 0)
    col = lax.broadcasted_iota(jnp.int32, (size, size), 1)
    return jnp.where(row + col == size - 1, 1.0, 0.0).astype(jnp.bfloat16)


def three_parts(values):
    high = values.astype(jnp.bfloat16)
    rest = values - high.astype(jnp.float32)
    middle = rest.astype(jnp.bfloat16)
    low = (rest - middle.astype(jnp.float32)).astype(jnp.bfloat16)
    return high, middle, low


def store_oriented(flags, planes, out, scale):
    count, rows, cols = planes.shape
    planes = scale * planes

    @pl.when(flags[1] == 0)
    def _():
        out[...] = planes

    @pl.when(flags[1] == 1)
    def _():
        flat = planes.reshape(count * rows, cols)
        matrix = exchange(cols)
        high, middle, low = (dot(part, matrix) for part in three_parts(flat))
        out[...] = ((high + middle) + low).reshape(count, rows, cols)

    @pl.when(flags[0] == 1)
    def _():
        matrix = exchange(rows)
        for n in range(count):
            high, middle, low = (dot(matrix, part) for part in three_parts(out[n]))
            out[n] = (high + middle) + low


def orient_kernel(scale, picks, flags, values, token, out, planes, sems):
    copies = []
    for n, (source, count, place) in enumerate(picks(flags)):
        copies.append(
            pltpu.make_async_copy(values.at[pl.ds(source, count)], planes.at[pl.ds(place, count)], sems.at[n])
        )
    for copy in copies:
        copy.start()
    for copy in copies:
        copy.wait()
    store_oriented(flags, planes[...], out, scale)


def orient_planes(values, flags, picks, runs, count, scale, token):
    shape = (count,) + values.shape[1:]
    anywhere, hbm = pl.BlockSpec(memory_space=pl.ANY), pl.BlockSpec(memory_space=pltpu.HBM)
    return pl.pallas_call(
        functools.partial(orient_kernel, scale, picks),
        out_shape=vmem_result(shape),
        in_specs=[pl.BlockSpec(memory_space=pltpu.SMEM), hbm, anywhere],
        out_specs=pl.BlockSpec(memory_space=pltpu.VMEM),
        scratch_shapes=[pltpu.VMEM(shape, jnp.float32), pltpu.SemaphoreType.DMA((runs,))],
        compiler_params=pltpu.CompilerParams(vmem_limit_bytes=16 << 20),
        cost_estimate=pl.CostEstimate(flops=count << 24, bytes_accessed=count << 19, transcendentals=0),
    )(flags, in_hbm(values), token)


def prepare_kernel(flags, signs, share, *refs):
    flow, viscosity, slope, own_y, own_z, sent, work, oriented, sems = refs[-9:]
    copies = (
        pltpu.make_async_copy(viscosity, work.at[0], sems.at[0]),
        pltpu.make_async_copy(slope, work.at[pl.ds(1, 2)], sems.at[1]),
        pltpu.make_async_copy(flow.at[pl.ds(1, 2)], work.at[pl.ds(3, 2)], sems.at[2]),
    )
    for copy in copies:
        copy.start()
    for copy in copies:
        copy.wait()
    for n in (1, 2):
        work[n] = signs[n] * (work[n] - work[n + 2])
    store_oriented(flags, work[0:3], oriented, 1.0)
    own_y[...] = oriented[0:2]
    own_z[0] = oriented[0]
    own_z[1] = oriented[2]
    rows = sent.shape[1]
    span = pl.ds(pl.multiple_of(share[0] * rows, rows), rows)
    for n in (0, 1):
        sent[n] = oriented[n, span, :]


def prepare(flags, signs, share, settled, share_rows, flow, viscosity, slope):
    rows, cols = viscosity.shape
    smem, hbm = pl.BlockSpec(memory_space=pltpu.SMEM), pl.BlockSpec(memory_space=pltpu.HBM)
    shapes = ((2, rows, cols), (2, rows, cols), (2, share_rows, cols))
    return pl.pallas_call(
        prepare_kernel,
        out_shape=tuple(vmem_result(s) for s in shapes),
        in_specs=[smem] * (3 + len(settled)) + [hbm] * 3,
        out_specs=(pl.BlockSpec(memory_space=pltpu.VMEM),) * 3,
        scratch_shapes=[
            pltpu.VMEM((5, rows, cols), jnp.float32),
            pltpu.VMEM((3, rows, cols), jnp.float32),
            pltpu.SemaphoreType.DMA((3,)),
        ],
        compiler_params=pltpu.CompilerParams(vmem_limit_bytes=10 << 20),
        cost_estimate=pl.CostEstimate(flops=1 << 26, bytes_accessed=3 << 20, transcendentals=0),
        name="prepare",
    )(flags, signs, share, *settled, in_hbm(flow), in_hbm(viscosity), in_hbm(slope))


def operator_kernel(variable, merged, layout, shares, spans, scalars, places, *refs):
    refs = list(refs)
    field, table_y, high_z, low_z = refs[:4]
    near_z, far_z, flows, own_y = refs[4:8]
    taken = 8
    plane = min(variable, 2)
    near_y, far_y = [None], []
    for b in range(spans):
        if b:
            near_y.append(refs[taken : taken + shares])
            taken += shares
        far_y.append(refs[taken : taken + shares])
        taken += shares
    taken += 1
    outs = refs[taken:-2]
    out_z = None if merged else outs[1]
    scratch_y, scratch_z = refs[-2:]

    rows, cols = field.shape[1:]
    half_rows = spans * rows
    half_cols = scratch_z.shape[2]
    share_rows = rows // shares
    stream, sign_y, sign_z = scalars[0], scalars[1], scalars[2]
    fold_y, fold_z = Y_SIGNS[variable], Z_SIGNS[variable]
    u, v, w, p = 0, 2, 4, 6
    base = 2 * variable
    step_y = min(ROW_STEP, share_rows)
    step_z = min(ROW_STEP, rows)

    def target(part, b):
        if layout == SLABS:
            return outs[b].at[part], 0
        first = pl.multiple_of(places[b], rows)
        return (outs[part].at[0] if layout == PARTS else outs[0].at[part]), first


    def along_y(part, source, kinds):
        high, low = split_high_low(field[source + part])
        stacked = jnp.concatenate((high, low, high, low), axis=0)

        @pl.loop(0, kinds // 2)
        def _(index):
            span = pl.ds(pl.multiple_of(index * 2 * half_rows, 2 * half_rows), 2 * half_rows)
            scratch_y[span, :] = dot(table_y[span, :], stacked)

    def along_z(source, kinds):
        both = field[source : source + 2].reshape(2 * rows, cols)
        high, low = split_high_low(both)

        @pl.loop(0, kinds)
        def _(kind):
            span = pl.ds(pl.multiple_of(kind * half_cols, half_cols), half_cols)
            total = dot(high, high_z[:, span])
            total = total + dot(low, high_z[:, span])
            total = total + dot(high, low_z[:, span])
            scratch_z[kind] = total

    def at(kind, start):
        return scratch_y[pl.ds(kind * half_rows + start, step_y), :]

    def rows_y(part, body):
        for b in range(spans):
            out, slab_first = target(part, b)

            @pl.loop(0, rows // step_y)
            def _(index, b=b, out=out, slab_first=slab_first):
                inner = pl.multiple_of(index * step_y, step_y)
                start = pl.multiple_of(places[b] + inner, step_y)
                body(out, pl.ds(pl.multiple_of(slab_first + inner, step_y), step_y), start)

    for part in (0, 1):
        if variable < 3:
            along_y(part, base, 4)
            for b in range(spans):
                for t in range(shares):
                    offset = pl.multiple_of(places[spans + t], share_rows)
                    out, slab_first = target(part, b)

                    @pl.loop(0, share_rows // step_y)
                    def _(index, b=b, t=t, offset=offset, out=out, slab_first=slab_first):
                        inner = pl.multiple_of(index * step_y, step_y)
                        start = pl.multiple_of(places[b] + offset + inner, step_y)
                        place = pl.multiple_of(slab_first + offset + inner, step_y)
                        local = pl.ds(inner, step_y)
                        if b:
                            viscous, slope = near_y[b][t][0, local, :], near_y[b][t][1, local, :]
                        else:
                            span = pl.ds(pl.multiple_of(offset + inner, step_y), step_y)
                            viscous, slope = own_y[0, span, :], own_y[1, span, :]
                        near = viscous * at(2, start) + slope * at(0, start)
                        far = far_y[b][t][0, local, :] * at(3, start) - far_y[b][t][1, local, :] * at(1, start)
                        out[pl.ds(place, step_y), :] = near + fold_y * far

            if variable == 1:
                along_y(part, p, 2)

                def push(out, span, start):
                    out[span, :] = out[span, :] - sign_y * (at(0, start) - at(1, start))

                rows_y(part, push)
        else:
            along_y(part, v, 2)

            def diverge(out, span, start):
                out[span, :] = sign_y * (at(0, start) + at(1, start))

            rows_y(part, diverge)

    def add_own(part, start, values):
        out, slab_first = target(part, 0)
        span = pl.ds(pl.multiple_of(slab_first + start, step_z), step_z)
        out[span, :] = out[span, :] + values

    def add_z(part, start, values):
        if merged:
            add_own(part, start, values)
        else:
            span = pl.ds(start, step_z)
            out_z[part, span, :] = out_z[part, span, :] + values

    if not merged:
        out_z[...] = jnp.zeros_like(out_z)

    def rows_z(body):
        @pl.loop(0, rows // step_z)
        def _(index):
            start = pl.multiple_of(index * step_z, step_z)
            for part in (0, 1):
                body(part, start)

    def at_z(kind, part, start):
        return scratch_z[kind, pl.ds(part * rows + start, step_z), :]

    def point(plane, start):
        return field[plane, pl.ds(start, step_z), :]

    turn = (1.0, -1.0)
    if variable < 3:
        along_z(base, 4)

        def both(part, start):
            span = pl.ds(start, step_z)
            near = near_z[0, span, :] * at_z(2, part, start) + near_z[1, span, :] * at_z(0, part, start)
            far = far_z[0, span, :] * at_z(3, part, start) - far_z[1, span, :] * at_z(1, part, start)
            add_z(part, start, near + fold_z * far)
            moved = turn[part] * stream * flows[0, span, :] * point(base + 1 - part, start)
            made = flows[1 + 2 * plane, span, :] * point(v + part, start) + flows[2 + 2 * plane, span, :] * point(w + part, start)
            lost = own_y[0, span, :] * (stream * stream) * point(base + part, start)
            values = moved - made - lost
            if variable == 0:
                values = values + turn[part] * stream * point(p + 1 - part, start)
            add_own(part, start, values)

        rows_z(both)
        if variable == 2:
            along_z(p, 2)

            def push_z(part, start):
                add_z(part, start, -sign_z * (at_z(0, part, start) - at_z(1, part, start)))

            rows_z(push_z)
    else:
        along_z(w, 2)

        def diverge_z(part, start):
            add_z(part, start, sign_z * (at_z(0, part, start) + at_z(1, part, start)))
            add_own(part, start, -turn[part] * stream * point(u + 1 - part, start))

        rows_z(diverge_z)


def call_in_vmem(kernel, out_shapes, scalars, arrays, token, flops, scratch=(), limit=8):
    vmem = pl.BlockSpec(memory_space=pltpu.VMEM)
    smem = pl.BlockSpec(memory_space=pltpu.SMEM)
    call = pl.pallas_call(
        kernel,
        out_shape=tuple(vmem_result(s) for s in out_shapes),
        in_specs=[smem] * len(scalars) + [vmem] * len(arrays) + [pl.BlockSpec(memory_space=pl.ANY)],
        out_specs=tuple(vmem for _ in out_shapes),
        scratch_shapes=list(scratch),
        compiler_params=pltpu.CompilerParams(vmem_limit_bytes=limit << 20),
        cost_estimate=pl.CostEstimate(flops=flops, bytes_accessed=3 << 20, transcendentals=0),
    )
    arrays = [in_vmem(a) for a in arrays]
    return call(*scalars, *arrays, token)


def apply_variable(variable, merged, layout, shares, half_cols, scalars, places, field, tables, coefs, token):
    near_z, far_z, flows, own_y, pieces = coefs
    rows, cols = field.shape[1:]
    half_rows = tables[0].shape[0] // 4
    spans = half_rows // rows
    shapes = {
        WHOLE: [(2, half_rows, cols)],
        PARTS: [(1, half_rows, cols)] * 2,
        SLABS: [(2, rows, cols)] * spans,
    }[layout]
    if not merged:
        shapes.append((2, rows, half_cols))
    work = 8 * 2 * (4 * half_rows * 4 * rows * cols + 3 * rows * cols * 4 * half_cols) // 4
    return call_in_vmem(
        functools.partial(operator_kernel, variable, merged, layout, shares, spans),
        shapes,
        (scalars, places),
        (field, *tables, near_z, far_z, flows, own_y, *pieces),
        token,
        work,
        (
            pltpu.VMEM((4 * half_rows, cols), jnp.float32),
            pltpu.VMEM((4, 2 * rows, half_cols), jnp.float32),
        ),
        20,
    )


def fold_kernel(sign, places, mine, theirs, token, kept, sent):
    rows = kept.shape[1]
    for part in range(mine.shape[0]):
        for slab, out in ((0, kept), (1, sent)):
            span = pl.ds(pl.multiple_of(places[slab], rows), rows)
            out[part] = mine[part, span, :] + sign * theirs[part, span, :]


def add_kernel(sign, mine, theirs, token, out):
    out[...] = mine[...] + sign * theirs[...]


def small_call(kernel, out_shapes, arrays, token, scalars=()):
    return call_in_vmem(kernel, out_shapes, scalars, arrays, token, 1 << 20)


def finish_kernel(sign, count, first, flags, *refs):
    kept, back, out, staged, sems = refs[:count], refs[count : 2 * count], refs[-3], refs[-2], refs[-1]
    for vector, (sources, factor) in enumerate(((kept, 1.0), (back, sign))):
        place = flags[1] if vector == 0 else 1 - flags[1]
        values = jnp.concatenate([ref[...] for ref in sources]) if count > 1 else sources[0][...]
        store_oriented(flags, values, staged.at[vector], factor)
        pltpu.make_async_copy(
            staged.at[vector], out.at[place, pl.ds(first, 2)], sems.at[vector]
        ).start()
    for vector in (0, 1):
        place = flags[1] if vector == 0 else 1 - flags[1]
        pltpu.make_async_copy(
            staged.at[vector], out.at[place, pl.ds(first, 2)], sems.at[vector]
        ).wait()


def finish(variable, flags, kept, back, response, token):
    rows, cols = kept[0].shape[1:]
    anywhere, vmem = pl.BlockSpec(memory_space=pl.ANY), pl.BlockSpec(memory_space=pltpu.VMEM)
    hbm = pl.BlockSpec(memory_space=pltpu.HBM)
    count = len(kept)
    arrays = [in_vmem(a) for a in (*kept, *back)]
    specs = [pl.BlockSpec(memory_space=pltpu.SMEM)] + [vmem] * len(arrays)
    extras = [token] if token is not response else []
    extras += [] if response is None else [in_hbm(response)]
    arrays += extras
    specs += [anywhere] * (len(extras) - 1) + [anywhere if response is None else hbm]
    return pl.pallas_call(
        functools.partial(finish_kernel, Z_SIGNS[variable], count, 2 * variable),
        out_shape=hbm_result((2, 8, rows, cols)),
        in_specs=specs,
        out_specs=hbm,
        scratch_shapes=[pltpu.VMEM((2, 2, rows, cols), jnp.float32), pltpu.SemaphoreType.DMA((2,))],
        input_output_aliases={} if response is None else {len(arrays): 0},
        compiler_params=pltpu.CompilerParams(vmem_limit_bytes=10 << 20),
        cost_estimate=pl.CostEstimate(flops=1 << 26, bytes_accessed=2 << 20, transcendentals=0),
    )(flags, *arrays)


def partner_pairs(size, bit, mirrored):
    pairs = []
    for i in range(size):
        far_end = i >= size // 2
        place = (size - 1 - i if far_end else i) ^ bit
        pairs.append((i, size - 1 - place if far_end != mirrored else place))
    return pairs


def halve(values, axis_name, position, dim):
    size = lax.axis_size(axis_name)
    bit = size // 4
    while bit:
        length = values.shape[dim] // 2
        upper = (position // bit) % 2
        kept = lax.dynamic_slice_in_dim(values, upper * length, length, dim)
        sent = lax.dynamic_slice_in_dim(values, (1 - upper) * length, length, dim)
        values = kept + lax.ppermute(sent, axis_name, partner_pairs(size, bit, False))
        bit //= 2
    return values


def gather_coefficients(planes, axis_name, flipped, dim):
    size = lax.axis_size(axis_name)
    gathered = lax.all_gather(planes, axis_name)
    low = jnp.concatenate([gathered[i] for i in range(size // 2)], axis=dim)
    high = jnp.concatenate([gathered[size - 1 - i] for i in range(size // 2)], axis=dim)
    return jnp.where(flipped, high, low), jnp.where(flipped, low, high)


def shards(forcing, wavenumber, mean_flow, viscosity, viscosity_slope):
    vectors, components, rows, cols = forcing.shape
    size_y, size_z, size_v = lax.axis_size("gy"), lax.axis_size("gz"), lax.axis_size("vec")
    half_rows, half_cols = rows * size_y // 2, cols * size_z // 2
    index_y, index_z = lax.axis_index("gy"), lax.axis_index("gz")
    flip_y = (index_y >= size_y // 2).astype(jnp.int32)
    flip_z = (index_z >= size_z // 2).astype(jnp.int32)
    place_y = jnp.where(flip_y == 1, size_y - 1 - index_y, index_y).astype(jnp.int32)
    place_z = jnp.where(flip_z == 1, size_z - 1 - index_z, index_z).astype(jnp.int32)
    sign_y = 1.0 - 2.0 * flip_y.astype(jnp.float32)
    sign_z = 1.0 - 2.0 * flip_z.astype(jnp.float32)
    flags = jnp.stack((flip_y, flip_z))
    merged = size_z == 2
    spans = size_y // 2
    half = vectors // 2

    shares = size_v if rows % (8 * size_v) == 0 else 1
    share_rows = rows // shares
    share = lax.axis_index("vec").astype(jnp.int32) if shares > 1 else jnp.int32(0)
    scalars = jnp.stack((wavenumber[0], sign_y, sign_z))
    places = jnp.stack(
        [(place_y ^ b) * rows for b in range(spans)]
        + [((share - k) % shares) * share_rows for k in range(shares)]
    )
    starts = jnp.stack((place_y * rows, place_z * cols))
    own_y, own_z, sent = prepare(
        flags, scalars, share[None], (places, starts), share_rows, mean_flow, viscosity, viscosity_slope
    )
    turn = [[(i, (i + k) % shares) for i in range(shares)] for k in range(shares)]
    pieces = []
    for b in range(spans):
        for mirrored in (False, True):
            if not b and not mirrored:
                continue
            got = lax.ppermute(sent, "gy", partner_pairs(size_y, b, mirrored))
            pieces += [got] + [lax.ppermute(got, "vec", turn[k]) for k in range(1, shares)]
    if merged:
        near_z, far_z = own_z, lax.ppermute(own_z, "gz", partner_pairs(size_z, 0, True))
    else:
        near_z, far_z = gather_coefficients(own_z, "gz", flip_z == 1, 2)
    tables = make_tables(rows, cols, half_rows, half_cols, starts, sent)
    planes = forcing.reshape(vectors * components, rows, cols)
    count = half * components

    def oriented(other, token):
        def picks(flags):
            which = 1 - flags[1] if other else flags[1]
            return [(which * count, count, 0)]

        return orient_planes(planes, flags, picks, 1, count, 0.25, token)

    sent_field = oriented(True, tables[0])
    flows = orient_planes(mean_flow, flags, lambda flags: [(0, 1, 0), (3, 6, 1)], 2, 7, 1.0, sent_field)
    kept_field = oriented(False, flows)
    coefs = (near_z, far_z, flows, own_y, pieces)

    def apply(variable, field, token, layout=WHOLE):
        return apply_variable(variable, merged, layout, shares, half_cols, scalars, places, field, tables, coefs, token)

    mirror_y, mirror_z = partner_pairs(size_y, 0, True), partner_pairs(size_z, 0, True)
    if merged and size_y == 4 and half == 1:
        return pipeline(apply, sent_field, kept_field, places, flags, mirror_y, mirror_z)

    def contribution(variable, field):
        parts = []
        for n in range(half):
            got = apply(variable, field[n * components : (n + 1) * components], scalars)
            if merged:
                parts.append(got[0])
            else:
                full = jnp.zeros((2, half_rows, half_cols), jnp.float32)
                full = lax.dynamic_update_slice_in_dim(full, got[0], place_z * cols, 2)
                start = place_y * rows
                strip = lax.dynamic_slice_in_dim(full, start, rows, 1) + got[1]
                parts.append(lax.dynamic_update_slice_in_dim(full, strip, start, 1))
        return halve(jnp.concatenate(parts), "gz", place_z, 2)

    kept_out, sent_out = [], []
    for variable in range(4):
        arrived = lax.ppermute(contribution(variable, sent_field), "gz", mirror_z)
        kept = contribution(variable, kept_field) + Z_SIGNS[variable] * arrived
        kept = halve(kept, "gy", place_y, 1)
        kept = kept + Y_SIGNS[variable] * lax.ppermute(kept, "gy", mirror_y)
        back = Z_SIGNS[variable] * lax.ppermute(kept, "gz", mirror_z)
        kept_out.append(kept.reshape(half, 2, rows, cols))
        sent_out.append(back.reshape(half, 2, rows, cols))
    kept = jnp.concatenate(kept_out, axis=1)
    back = jnp.concatenate(sent_out, axis=1)
    first = jnp.where(flip_z == 1, back, kept)
    second = jnp.where(flip_z == 1, kept, back)
    both = jnp.concatenate((first, second)).reshape(vectors * components, rows, cols)
    every = lambda flags: [(0, vectors * components, 0)]
    out = orient_planes(both, flags, every, 1, vectors * components, 1.0, scalars)
    return out.reshape(forcing.shape)


def add_all_kernel(sign, mine, near, theirs, token, out):
    out[...] = (mine[...] + near[...]) + sign * theirs[...]


def pipeline(apply, sent_field, kept_field, places, flags, mirror_y, mirror_z):
    rows, cols = sent_field.shape[1:]
    neighbour_y = partner_pairs(4, 1, False)
    token = kept_field
    kept, moving, extra, sends = {}, {}, {}, []
    response = None

    def chunks(n):
        return ((n, 0), (n, 1)) if LAYOUT[n] == PARTS else ((n, 0),)

    def send(values, axis, partners):
        sends[-1].append(axis)
        return lax.ppermute(values, axis, partners)

    def add(kernel, arrays, shape):
        return small_call(kernel, (shape,), arrays, token)[0]

    def act(step, key):
        nonlocal token, response
        n = key[0]
        if step in "SK":
            parts = apply(n, sent_field if step == "S" else kept_field, token, LAYOUT[n])
            token = parts[0]
            if LAYOUT[n] == SLABS:
                arrived = send(parts[1], "gy", neighbour_y)
                (extra if step == "S" else kept)[key] = (parts[0], arrived)
                return
            for chunk, part in zip(chunks(n), parts):
                if step == "S":
                    moving[chunk] = send(part, "gz", mirror_z)
                else:
                    kept[chunk] = part
            return
        if step == "W":
            sources = [kept[c] for c in chunks(n)], [moving[c] for c in chunks(n)]
            response = token = finish(n, flags, *sources, response, token)
            return
        if step == "A":
            token = add(functools.partial(add_kernel, 1.0), extra[key], extra[key][0].shape)
            moving[key] = send(token, "gz", mirror_z)
            return
        if step == "C":
            arrays = (*kept[key], moving[key])
            token = add(functools.partial(add_all_kernel, Z_SIGNS[n]), arrays, arrays[0].shape)
            kept[key] = token
            moving[key] = send(token, "gy", mirror_y)
            return
        small = (kept[key].shape[0], rows, cols)
        pair = (kept[key], moving[key])
        if step == "X":
            kept[key], token = small_call(
                functools.partial(fold_kernel, Z_SIGNS[n]), (small, small), pair, token, (places,)
            )
            moving[key] = send(token, "gy", neighbour_y)
        else:
            sign, axis, partners = (1.0, "gy", mirror_y) if step == "Y" else (Y_SIGNS[n], "gz", mirror_z)
            token = add(functools.partial(add_kernel, sign), pair, small)
            kept[key] = token
            moving[key] = send(token, axis, partners)

    for step, *key in ORDER:
        sends.append([])
        act(step, tuple(key))
    return response


LAYOUT = (PARTS, PARTS, PARTS, PARTS)
ORDER = (
    ("S", 3, 0), ("S", 0, 0), ("K", 3, 0), ("X", 3, 0), ("S", 2, 0), ("Y", 3, 0),
    ("X", 3, 1), ("K", 0, 0), ("X", 0, 0), ("Y", 3, 1), ("S", 1, 0), ("Y", 0, 0),
    ("X", 0, 1), ("K", 2, 0), ("X", 2, 0), ("Y", 0, 1), ("X", 2, 1), ("K", 1, 0),
    ("Y", 2, 0), ("X", 1, 0), ("M", 3, 0), ("M", 0, 0), ("M", 0, 1), ("Y", 2, 1),
    ("X", 1, 1), ("M", 3, 1), ("Y", 1, 0), ("M", 2, 0), ("W", 0), ("Y", 1, 1),
    ("M", 2, 1), ("W", 3), ("M", 1, 0), ("M", 1, 1), ("W", 2), ("W", 1),
)


def solution(mesh):
    placed = (
        P(("wave", "vec"), None, "gy", "gz"),
        P("wave"),
        P(None, "gy", "gz"),
        P("gy", "gz"),
        P(None, "gy", "gz"),
    )

    return jax.shard_map(
        shards,
        mesh=mesh,
        in_specs=placed,
        out_specs=P(("wave", "vec"), None, "gy", "gz"),
        check_vma=False,
    )
```
